512 devices in a mesh: head: 8 (over y_hi, x), blk: 64 (over y_lo, z, core).
Axes of the slice: x: 4, y: 8 (y_hi: 2, y_lo: 4; y = y_hi * 4 + y_lo), z: 8, core: 2. Of those that a mesh axis runs over, the one named last changes fastest.
Arguments:
- query_rows: bfloat16 [8192, 1536], P(('head', 'blk')), may hold values from -400 to 400
- key_rows: bfloat16 [8192, 1536], P(('head', 'blk')), may hold values from -400 to 400
- value_rows: bfloat16 [8192, 1536], P(('head', 'blk')), may hold values from -6 to 6
- residual: bfloat16 [8192, 1536], P(('head', 'blk')), may hold values from -6 to 6
- out_weight: bfloat16 [1536, 1536], P('head'), may hold values from -0.15625 to 0.15625
- attention_gate: float32 [1536], replicated, may hold values from 0.5 to 1.5
- norm_shift: float32 [1536], replicated, may hold values from -1 to 1
- norm_scale: float32 [1536], replicated, may hold values from -0.5 to 0.5
- expert_gate: float32 [1536], replicated, may hold values from 0.5 to 1.5
- expert_up: bfloat16 [64, 1536, 4096], P('blk', None, 'head'), may hold values from -0.15625 to 0.15625
- expert_down: bfloat16 [64, 4096, 1536], P('blk', 'head'), may hold values from -0.09375 to 0.09375
- routing: int32 [8192, 2], P(('head', 'blk')), may hold values from 0 to 63, as said below
- combine_weight: float32 [8192, 2], P(('head', 'blk')), may hold values from 0.2 to 1
Outputs:
- mixed: bfloat16 [8192, 1536], P(('head', 'blk'))
The draws below stay inside these ranges and needn't reach their ends.
Inputs may be any that keep to these rules, and one draw needn't show every extreme that they name: `routing`: the two choices of a token differ. Within the 16 tokens of one device every expert is named at most 2 times, and one expert, the same for every device, is named exactly 2 times by every device.
All inputs are finite; a program needn't handle non-finite values.
Results may differ from the reference program's by a relative error of at most 0.011.
Values may be sent and summed in bfloat16 or wider, within the bound.
No kernel may reach another device: no remote copies, remote signals or barrier semaphores. Data moves between devices by JAX's collectives and lax.ppermute only.
A program may use at most 64 MiB of HBM per device.

```python
import math
import jax
import jax.numpy as jnp
from jax import lax

D = 1536
HEADS = 24
HD = 64
FF = 4096
TOPK = 2
TOK_DEV = 16
CAP = 2
TOKENS = 8192
EXPERTS = 64
N_HEAD = 8
N_BLK = 64


def draw_query_rows(key, part):
    base = jnp.clip(jax.random.normal(jax.random.fold_in(key, 1), (TOKENS, D)) * 2.5, -15.0, 15.0)
    return base.astype(jnp.bfloat16)


def draw_key_rows(key, part):
    base = jnp.clip(jax.random.normal(jax.random.fold_in(key, 2), (TOKENS, D)), -6.0, 6.0)
    return base.astype(jnp.bfloat16)


def draw_routing(key, part):
    hot_expert = jax.random.randint(jax.random.fold_in(key, 31), (), 0, EXPERTS).astype(jnp.int32)
    block_total = TOKENS // TOK_DEV
    keys_perm = jax.random.split(jax.random.fold_in(key, 32), block_total)
    keys_order = jax.random.split(jax.random.fold_in(key, 33), block_total)
    keys_side = jax.random.split(jax.random.fold_in(key, 34), block_total)

    def one_block(key_perm, key_order, key_side):
        shuffled = jax.random.permutation(key_perm, EXPERTS - 1).astype(jnp.int32)
        others = shuffled + (shuffled >= hot_expert).astype(jnp.int32)
        repeated = jnp.tile(others, CAP)
        sequence = jnp.concatenate([jnp.full((CAP,), hot_expert, jnp.int32), repeated])[:TOPK * TOK_DEV]
        first_choice = sequence[:TOK_DEV]
        second_choice = sequence[TOK_DEV:TOPK * TOK_DEV]
        swapped = jax.random.randint(key_side, (TOK_DEV,), 0, 2)
        left_side = jnp.where(swapped == 1, second_choice, first_choice)
        right_side = jnp.where(swapped == 1, first_choice, second_choice)
        paired = jnp.stack([left_side, right_side], axis=1)
        row_order = jax.random.permutation(key_order, TOK_DEV)
        return paired[row_order]
    return jax.vmap(one_block)(keys_perm, keys_order, keys_side).reshape(TOKENS, TOPK).astype(jnp.int32)


def steps_of(key, dims, cuts, smallest, top_value):
    level = 1.0
    for dim, blocks in cuts:
        draws = jax.random.uniform(jax.random.fold_in(jax.random.fold_in(key, 6), dim), (blocks,), jnp.float32, smallest / len(cuts), top_value / len(cuts))
        level = level * jnp.repeat(jnp.exp(draws), dims[dim] // blocks).reshape((-1,) + (1,) * (len(dims) - 1 - dim))
    return level


def centred(key, shape, spread, limit, shards=(), kind=jnp.bfloat16):
    array = spread * jax.random.normal(key, shape, jnp.float32)
    if shards:
        array = array * steps_of(key, shape, shards, -0.22, 0.18)
    return jnp.clip(array, -limit, limit).astype(kind)


def setup_inputs(seed: int = 0) -> dict:
    streams_of = jax.random.split(jax.random.key(seed), 14)
    query_rows = draw_query_rows(jax.random.fold_in(streams_of[13], 71), 0)
    key_rows = draw_key_rows(jax.random.fold_in(streams_of[13], 71), 0)
    value_rows = centred(streams_of[2], (TOKENS, D), 1.0, 6.0, ((0, 512),))
    residual = centred(streams_of[3], (TOKENS, D), 1.0, 6.0, ((0, 512),))
    out_weight = centred(streams_of[4], (D, D), D ** -0.5, 0.15625, ((0, 8),))
    attention_gate = jnp.clip(jax.random.uniform(streams_of[5], (D,), jnp.float32, 0.5, 1.5), 0.5, 1.5)
    norm_shift = jnp.clip(jax.random.uniform(streams_of[6], (D,), jnp.float32, -1.0, 1.0), -1.0, 1.0)
    norm_scale = jnp.clip(jax.random.uniform(streams_of[7], (D,), jnp.float32, -0.5, 0.5), -0.5, 0.5)
    expert_gate = jnp.clip(jax.random.uniform(streams_of[8], (D,), jnp.float32, 0.5, 1.5), 0.5, 1.5)
    expert_up = centred(streams_of[9], (EXPERTS, D, FF), D ** -0.5, 0.15625, ((0, 64), (2, 8)))
    expert_down = centred(streams_of[10], (EXPERTS, FF, D), FF ** -0.5, 0.09375, ((0, 64), (1, 8)))
    routing = draw_routing(jax.random.fold_in(streams_of[13], 71), 0)
    combine_weight = jnp.clip(0.2 + 0.8 * jax.random.uniform(streams_of[12], (TOKENS, TOPK), jnp.float32) ** steps_of(streams_of[12], (TOKENS, TOPK), ((0, 512),), -0.2, 0.2), 0.2, 1.0)
    return {"query_rows": query_rows, "key_rows": key_rows, "value_rows": value_rows, "residual": residual, "out_weight": out_weight, "attention_gate": attention_gate, "norm_shift": norm_shift, "norm_scale": norm_scale, "expert_gate": expert_gate, "expert_up": expert_up, "expert_down": expert_down, "routing": routing, "combine_weight": combine_weight}


def one_head(operands):
    query_head, key_head, value_head = operands
    scores = jnp.dot(query_head, key_head.T, preferred_element_type=jnp.float32) * (1.0 / math.sqrt(HD))
    peak = lax.optimization_barrier(jnp.max(scores, axis=1, keepdims=True))
    probs = jnp.exp(scores - peak)
    denom = lax.optimization_barrier(jnp.sum(probs, axis=1, keepdims=True))
    numer = jnp.dot(probs.astype(jnp.bfloat16), value_head, preferred_element_type=jnp.float32)
    return numer / denom

def reference(query_rows, key_rows, value_rows, residual, out_weight, attention_gate, norm_shift, norm_scale, expert_gate, expert_up, expert_down, routing, combine_weight):
    total_rows = query_rows.shape[0]

    def split_heads(matrix):
        return matrix.reshape(total_rows, HEADS, HD).transpose(1, 0, 2)
    per_head = lax.map(one_head, (split_heads(query_rows), split_heads(key_rows), split_heads(value_rows)))
    attended = per_head.transpose(1, 0, 2).reshape(total_rows, D).astype(jnp.bfloat16)
    group_width = D // N_HEAD
    projected = jnp.zeros((total_rows, D), jnp.float32)
    for group in range(N_HEAD):
        part_sum = jnp.dot(attended[:, group * group_width:(group + 1) * group_width], out_weight[group * group_width:(group + 1) * group_width], preferred_element_type=jnp.float32).astype(jnp.bfloat16)
        projected = projected + lax.optimization_barrier(part_sum).astype(jnp.float32)
    middle = residual.astype(jnp.float32) + attention_gate * projected
    average = lax.optimization_barrier(jnp.mean(middle, axis=1, keepdims=True))
    centered = middle - average
    variance = lax.optimization_barrier(jnp.mean(centered * centered, axis=1, keepdims=True))
    normed = (centered * lax.rsqrt(variance + 1e-06) * (1.0 + norm_scale) + norm_shift).astype(jnp.bfloat16)
    entries = routing.reshape(-1).astype(jnp.int32)
    entry_count = entries.shape[0]
    devices_all = N_HEAD * N_BLK
    per_source = entries.reshape(devices_all, TOPK * TOK_DEV)
    onehot = (per_source[:, :, None] == jnp.arange(EXPERTS, dtype=jnp.int32)[None, None, :]).astype(jnp.int32)
    before = jnp.cumsum(onehot, axis=1) - onehot
    slot_number = lax.optimization_barrier(jnp.sum(before * onehot, axis=2)).reshape(-1).astype(jnp.int32)
    source = jnp.arange(entry_count, dtype=jnp.int32) // (TOPK * TOK_DEV)
    position = (source * CAP + slot_number).astype(jnp.int32)
    buffer_rows = devices_all * CAP
    ff_group = FF // N_HEAD

    def one_expert(results, expert):
        chosen = entries == expert
        target = jnp.where(chosen, position, buffer_rows).astype(jnp.int32)
        entry_of_slot = jnp.zeros((buffer_rows,), jnp.int32).at[target].set(jnp.arange(entry_count, dtype=jnp.int32), mode='drop')
        rows_in = normed[entry_of_slot // TOPK]
        hidden = jax.nn.gelu(jnp.dot(rows_in, expert_up[expert], preferred_element_type=jnp.float32), approximate=True).astype(jnp.bfloat16)
        down_here = expert_down[expert]
        summed = jnp.zeros((buffer_rows, D), jnp.float32)
        for group in range(N_HEAD):
            part_sum = jnp.dot(hidden[:, group * ff_group:(group + 1) * ff_group], down_here[group * ff_group:(group + 1) * ff_group], preferred_element_type=jnp.float32).astype(jnp.bfloat16)
            summed = summed + lax.optimization_barrier(part_sum).astype(jnp.float32)
        expert_out = summed.astype(jnp.bfloat16)
        return (jnp.where(chosen[:, None], expert_out[position], results), None)
    results, _ = lax.scan(one_expert, jnp.zeros((entry_count, D), jnp.bfloat16), jnp.arange(EXPERTS, dtype=jnp.int32))
    mixture = lax.optimization_barrier(jnp.sum(results.reshape(total_rows, TOPK, D).astype(jnp.float32) * combine_weight[:, :, None], axis=1))
    return (middle + expert_gate * mixture).astype(jnp.bfloat16)
```

```python
import math

import jax
import jax.numpy as jnp
from jax import lax
from jax.sharding import Mesh
from jax.sharding import PartitionSpec as P

HD = 64
TOPK = 2
SLOTS = 2
AXES = ("yh", "x", "yl", "z", "c")
HEAD = ("yh", "x")
BLK = ("yl", "z", "c")


def exchange(array, axis):
    return lax.all_to_all(array, axis, 0, 0, tiled=True)


def gathered(array, axis):
    copies = jnp.broadcast_to(array[None], (lax.axis_size(axis), *array.shape))
    return exchange(copies, axis)


def partner(array, axis):
    return lax.ppermute(array, axis, [(0, 1), (1, 0)])


def both_sides(array, axis):
    other = partner(array, axis)
    first = lax.axis_index(axis) == 0
    return jnp.stack([jnp.where(first, array, other), jnp.where(first, other, array)])


def in_pieces(values, count):
    pieces = []
    for _ in range(count):
        piece = lax.reduce_precision(values, 8, 7)
        pieces.append(piece)
        values = values - piece
    return pieces


def on_device(
    query_rows,
    key_rows,
    value_rows,
    residual,
    out_weight,
    attention_gate,
    norm_shift,
    norm_scale,
    expert_gate,
    expert_up,
    expert_down,
    routing,
    combine_weight,
):
    bf16, f32 = jnp.bfloat16, jnp.float32
    tok, width = query_rows.shape
    n_head = lax.axis_size(HEAD)
    n_x = lax.axis_size("x")
    n_z = lax.axis_size("z")
    experts = lax.axis_size(BLK)
    cols = width // n_head
    heads = cols // HD
    rows = n_head * tok

    residual_both = both_sides(residual, "yh").reshape(2 * tok, width)
    routed = jnp.concatenate([routing.astype(f32), combine_weight], axis=1)
    routed_both = both_sides(routed, "yh")
    choice = routed_both[:, :, :TOPK].astype(jnp.int32)
    weight = routed_both[:, :, TOPK:].reshape(2 * tok, TOPK)

    own = jnp.concatenate(
        [a.reshape(tok, n_head, cols) for a in (query_rows, key_rows, value_rows)], axis=2
    )
    own = exchange(jnp.transpose(own, (1, 0, 2)), HEAD).reshape(rows, 3 * cols)
    keys_values = gathered(own[:, cols:], "yl").reshape(-1, 2 * cols)
    keys_values = jnp.concatenate([keys_values, partner(keys_values, "c")], axis=0)
    queries = gathered(own[:, :cols], "z").reshape(-1, cols)

    q = queries.reshape(-1, heads, HD)
    k = keys_values[:, :cols].reshape(-1, heads, HD)
    v = keys_values[:, cols:].reshape(-1, heads, HD)
    scores = jnp.einsum("rhd,phd->hrp", q, k, preferred_element_type=f32) * (1.0 / math.sqrt(HD))
    peak = jnp.max(scores, axis=2)
    probs = jnp.exp(scores - peak[:, :, None])
    total = jnp.sum(probs, axis=2)
    accum = jnp.einsum("hrp,phd->hrd", probs.astype(bf16), v, preferred_element_type=f32)
    part = (accum / total[:, :, None]).astype(bf16)
    part = jnp.transpose(part, (1, 0, 2)).reshape(-1, cols)
    stats = jnp.concatenate(in_pieces(peak, 3) + in_pieces(total, 3), axis=0).astype(bf16).T
    stats = jnp.pad(stats, ((0, 0), (0, 64 - stats.shape[1])))
    packed = jnp.concatenate([part, stats], axis=1).reshape(n_z, rows, cols + 64)
    packed = exchange(packed, "z")
    parts = packed[:, :, :cols].astype(f32).reshape(n_z, rows, heads, HD)
    stats = packed[:, :, cols : cols + 6 * heads].astype(f32).reshape(n_z, rows, 6, heads)
    peaks = jnp.sum(stats[:, :, :3], axis=2)
    totals = jnp.sum(stats[:, :, 3:], axis=2)
    share = totals * jnp.exp(peaks - jnp.max(peaks, axis=0, keepdims=True))
    share = share / jnp.sum(share, axis=0, keepdims=True)
    attended = jnp.sum(parts * share[:, :, :, None], axis=0).reshape(rows, cols).astype(bf16)

    partial = jnp.dot(attended, out_weight, preferred_element_type=f32).astype(bf16)
    partial = partial.reshape(2, n_x, tok, width).transpose(1, 0, 2, 3).reshape(n_x, 2 * tok, width)
    summed = jnp.sum(exchange(partial, "x").astype(f32), axis=0)
    projected = summed + partner(summed.astype(bf16), "yh").astype(f32)

    middle = residual_both.astype(f32) + attention_gate * projected
    average = jnp.mean(middle, axis=1, keepdims=True)
    centered = middle - average
    variance = jnp.mean(centered * centered, axis=1, keepdims=True)
    normed = (centered * lax.rsqrt(variance + 1e-06) * (1.0 + norm_scale) + norm_shift).astype(bf16)

    flat = choice.reshape(2, -1)
    same = flat[:, :, None] == flat[:, None, :]
    order = jnp.arange(flat.shape[1])
    earlier = same & (order[None, None, :] < order[None, :, None])
    slot = jnp.sum(earlier.astype(jnp.int32), axis=2)
    source = jnp.arange(2, dtype=jnp.int32)[:, None]
    place = ((flat * 2 + source) * SLOTS + slot).reshape(2 * tok, TOPK)
    per_expert = 2 * SLOTS
    buffer_rows = experts * per_expert
    hit = place[:, :, None] == jnp.arange(buffer_rows, dtype=jnp.int32)[None, None, :]
    chosen = jnp.any(hit, axis=1).astype(bf16)
    sent = jnp.dot(chosen.T, normed, preferred_element_type=f32).astype(bf16)
    arrived = exchange(sent.reshape(experts, per_expert, width), BLK).reshape(buffer_rows, width)

    buffers = gathered(arrived, "x").reshape(n_x * buffer_rows, width)
    hidden = jax.nn.gelu(
        jnp.dot(buffers, expert_up[0], preferred_element_type=f32), approximate=True
    ).astype(bf16)
    output = jnp.dot(hidden, expert_down[0], preferred_element_type=f32).astype(bf16)
    output = exchange(output.reshape(n_x, buffer_rows, width), "x")
    output = jnp.sum(output.astype(f32), axis=0).astype(bf16)
    returned = exchange(output.reshape(experts, per_expert, width), BLK).reshape(buffer_rows, width)

    pick = jnp.sum(jnp.where(hit, weight[:, :, None], 0.0), axis=1)
    pick = jnp.concatenate(in_pieces(pick, 2), axis=0).astype(bf16)
    mixed = jnp.dot(pick, returned, preferred_element_type=f32).reshape(2, 2, tok, width)
    mixed = mixed[0] + mixed[1]
    side = lax.axis_index("yh") == 0
    kept = jnp.where(side, mixed[0], mixed[1])
    given = jnp.where(side, mixed[1], mixed[0]).astype(bf16)
    mixture = kept + partner(given, "yh").astype(f32)
    middle = middle.reshape(2, tok, width)
    middle = jnp.where(side, middle[0], middle[1])
    return (middle + expert_gate * mixture).astype(bf16)


def solution(mesh):
    split = Mesh(mesh.devices.reshape(2, 4, 4, 8, 2), AXES)
    everywhere = P(AXES, None)
    placed = (
        everywhere,
        everywhere,
        everywhere,
        everywhere,
        P(HEAD, None),
        P(),
        P(),
        P(),
        P(),
        P(BLK, None, HEAD),
        P(BLK, HEAD, None),
        everywhere,
        everywhere,
    )
    return jax.shard_map(
        on_device, mesh=split, in_specs=placed, out_specs=everywhere, check_vma=False
    )
```

```python
import math

import jax
import jax.numpy as jnp
from jax import lax
from jax.experimental import pallas as pl
from jax.experimental.pallas import tpu as pltpu
from jax.sharding import Mesh
from jax.sharding import PartitionSpec as P

HD = 64
TOPK = 2
SLOTS = 2
FEW = 96
LANES = 128
AXES = ("yh", "x", "yl", "z", "c")
HEAD = ("yh", "x")
BLK = ("yl", "z", "c")
PLANE = ("yl", "z")
BF16 = jnp.bfloat16
F32 = jnp.float32
RATE = math.log2(math.e) / math.sqrt(HD)


def exchange(array, axis):
    return lax.all_to_all(array, axis, 0, 0, tiled=True)


def gathered(array, axis):
    copies = jnp.broadcast_to(array[None], (lax.axis_size(axis), *array.shape))
    return exchange(copies, axis)


def partner(array, axis):
    return lax.ppermute(array, axis, [(0, 1), (1, 0)])


def shifted(array, by):
    n = lax.axis_size("x")
    return lax.ppermute(array, "x", [(i, (i + by) % n) for i in range(n)])


def iota(shape, dim):
    return lax.broadcasted_iota(jnp.int32, shape, dim)


def dot(a, b, dims=((1,), (0,))):
    return lax.dot_general(a, b, (dims, ((), ())), preferred_element_type=F32)


def pieces(values):
    out = []
    for _ in range(3):
        piece = values.astype(BF16).astype(F32)
        out.append(piece)
        values = values - piece
    return out


def local(body, outs, *args, name, smem=(), **kw):
    specs = [
        pl.BlockSpec(memory_space=pltpu.SMEM if i in smem else pltpu.VMEM)
        for i in range(len(args))
    ]
    return pl.pallas_call(
        body,
        out_shape=outs,
        in_specs=specs,
        out_specs=jax.tree.map(lambda _: pl.BlockSpec(memory_space=pltpu.VMEM), outs),
        name=name,
        **kw,
    )(*args)


def shape(dims, kind=BF16):
    return jax.ShapeDtypeStruct(dims, kind)


def prepare(q_ref, k_ref, v_ref, route_ref, weight_ref, out_ref):
    groups, tok, _ = out_ref.shape
    cols = q_ref.shape[1] // groups
    weight = weight_ref[...]
    lines = [route_ref[k : k + 1, :].astype(F32) for k in range(TOPK)]
    for piece in pieces(weight):
        lines += [piece[k : k + 1, :] for k in range(TOPK)]
    row = iota((16, tok), 0)
    table = jnp.zeros((16, tok), F32)
    for i, line in enumerate(lines):
        table = jnp.where(row == i, line, table)
    pick = (iota((16, HD), 0) == iota((16, HD), 1)).astype(BF16)
    header = dot(table.astype(BF16), pick, ((0,), (0,))).astype(BF16)
    for g in range(groups):
        span = slice(g * cols, (g + 1) * cols)
        out_ref[g] = jnp.concatenate(
            [q_ref[:, span], header, k_ref[:, span], v_ref[:, span]], axis=1
        )


def attend(q_ref, near_ref, far_ref, out_ref):
    rows, cols = q_ref.shape
    heads = cols // HD
    q = q_ref[...]
    near_k, far_k = near_ref[:, :cols], far_ref[:, :cols]
    near_v, far_v = near_ref[:, LANES:], far_ref[:, LANES:]
    q_head = iota((rows, cols), 1) // HD
    lane = iota((rows, cols + HD), 1)
    out = jnp.zeros((rows, cols + HD), F32)
    for j in range(heads):
        q_j = jnp.where(q_head == j, q, jnp.zeros_like(q))
        near = dot(q_j, near_k, ((1,), (1,)))
        far = dot(q_j, far_k, ((1,), (1,)))
        peak = jnp.maximum(
            jnp.max(near, axis=1, keepdims=True), jnp.max(far, axis=1, keepdims=True)
        )
        near = jnp.exp2((near - peak) * RATE)
        far = jnp.exp2((far - peak) * RATE)
        total = jnp.sum(near, axis=1, keepdims=True) + jnp.sum(far, axis=1, keepdims=True)
        accum = dot(near.astype(BF16), near_v) + dot(far.astype(BF16), far_v)
        out = jnp.where(lane // HD == j + 1, accum * (1.0 / total), out)
        for i, piece in enumerate(pieces(peak) + pieces(total)):
            out = jnp.where(lane == 6 * j + i, piece, out)
    out_ref[...] = out.astype(BF16)


def project(parts_ref, weight_ref, out_ref):
    count, rows, wide = parts_ref.shape
    n_x, pair_rows, _ = out_ref.shape
    tok = pair_rows // 2
    stats = parts_ref[:, :, :LANES].reshape(count * rows, LANES)
    src = iota((LANES, wide), 0)
    head = jnp.maximum(iota((LANES, wide), 1) // HD - 1, 0)
    at = src - 6 * head
    peak = dot(stats, ((at >= 0) & (at < 3)).astype(BF16)).reshape(count, rows, wide)
    total = dot(stats, ((at >= 3) & (at < 6)).astype(BF16)).reshape(count, rows, wide)
    top = jnp.max(peak, axis=0)
    share = total * jnp.exp2((peak - top[None]) * RATE)
    numer = jnp.sum(share * parts_ref[...].astype(F32), axis=0)
    attended = (numer / jnp.sum(share, axis=0))[:, HD:].astype(BF16)
    projected = dot(attended, weight_ref[...]).astype(BF16)
    for side in range(2):
        for x in range(n_x):
            start = (side * n_x + x) * tok
            out_ref[x, side * tok : (side + 1) * tok, :] = projected[start : start + tok]


def sum_pair(where_ref, parts_ref, residual_ref, gate_ref, sum_ref, out_ref):
    tok = residual_ref.shape[0]
    total = parts_ref[0].astype(F32)
    for x in range(1, parts_ref.shape[0]):
        total = total + parts_ref[x].astype(F32)
    total = total * gate_ref[...]
    sum_ref[...] = total
    own = where_ref[0]
    residual = residual_ref[...].astype(F32)
    for side in range(2):
        span = slice(side * tok, (side + 1) * tok)
        added = jnp.where(own == side, residual, 0.0)
        out_ref[span, :] = (total[span] + added).astype(BF16)


def normalize(
    where_ref, sum_ref, got_ref, residual_ref, shift_ref, scale_ref, own_ref, middle_ref, out_ref
):
    tok, width = residual_ref.shape
    own = where_ref[0]
    residual = residual_ref[...].astype(F32)
    for side in range(2):
        span = slice(side * tok, (side + 1) * tok)
        added = jnp.where(own == side, residual, 0.0)
        middle = sum_ref[span, :] + got_ref[span, :].astype(F32) + added

        @pl.when(own == side)
        def _():
            middle_ref[...] = middle

        average = jnp.mean(middle, axis=1, keepdims=True)
        centered = middle - average
        variance = jnp.mean(centered * centered, axis=1, keepdims=True)
        scaled = centered * lax.rsqrt(variance + 1e-06) * (1.0 + scale_ref[...])
        out_ref[span, :width] = (scaled + shift_ref[...]).astype(BF16)
    both = 2 * tok
    for i in range(own_ref.shape[0] // both):
        start = width + i * LANES
        out_ref[:, start : start + LANES] = own_ref[i * both : (i + 1) * both, LANES : 2 * LANES]


def headers_of(near_ref, far_ref, width):
    rows = []
    for ref in (near_ref, far_ref):
        for i in range((ref.shape[1] - width) // LANES):
            start = width + i * LANES
            rows.append(ref[:, start : start + LANES])
    return jnp.concatenate(rows, axis=0)


def ours_of(headers, x, tok, n_x):
    count = 4 * tok
    row, col = iota((count, headers.shape[0]), 0), iota((count, headers.shape[0]), 1)
    wanted = ((row // tok) * n_x + x) * tok + row % tok
    return dot((col == wanted).astype(BF16), headers).astype(BF16)


def dispatch(where_ref, near_ref, far_ref, out_ref, *, width, n_x):
    pair = near_ref.shape[0]
    tok = pair // 2
    x, c = where_ref[1], where_ref[2]
    rows = out_ref.shape[0]
    per_expert = 4 * SLOTS
    headers = headers_of(near_ref, far_ref, width)
    ours = ours_of(headers, x, tok, n_x)
    count = ours.shape[0]
    take = (iota((8, LANES), 1) == iota((8, LANES), 0) + HD).astype(BF16)
    line = dot(take, ours, ((1,), (1,)))
    col = [jnp.sum(jnp.where(iota((count, LANES), 1) == HD + k, ours.astype(F32), 0.0), axis=1, keepdims=True) for k in range(TOPK)]
    first, second = iota((count, count), 0), iota((count, count), 1)
    before = (first < second) & (first // tok == second // tok)
    hits = jnp.zeros((rows, count), F32)
    target = iota((rows, count), 0)
    group = iota((1, count), 1) // tok
    for k in range(TOPK):
        named = line[k : k + 1, :]
        same = sum((col[m] == named).astype(F32) for m in range(TOPK))
        slot = jnp.sum(jnp.where(before, same, 0.0), axis=0, keepdims=True).astype(jnp.int32)
        expert = named.astype(jnp.int32)
        place = (expert // 2) * per_expert + group * SLOTS + slot
        place = jnp.where(expert % 2 == c, place, -1)
        hits = hits + (target == place).astype(F32)
    onehot = hits.astype(BF16)
    out_ref[:, :width] = (
        dot(onehot[:, :pair], near_ref[:, :width]) + dot(onehot[:, pair:], far_ref[:, :width])
    ).astype(BF16)
    every = headers.shape[0]
    lines = dot(take, headers, ((1,), (1,)))
    named_here = (iota((rows, every), 0) // per_expert * 2 + c).astype(F32)
    named = sum((lines[k : k + 1, :] == named_here).astype(F32) for k in range(TOPK))
    member = (iota((every, LANES), 0) // tok % n_x == iota((every, LANES), 1)).astype(BF16)
    counts = dot(named.astype(BF16), member)
    filled = jnp.sum(hits, axis=1, keepdims=True)
    marks = jnp.where(iota((rows, LANES), 1) == n_x, filled, counts)
    out_ref[:, width:] = marks.astype(BF16)


def mix(where_ref, near_ref, far_ref, rows_ref, kept_ref, given_ref, *, width, n_x):
    pair = near_ref.shape[0]
    tok = pair // 2
    x, c = where_ref[1], where_ref[2]
    rows = rows_ref.shape[0]
    per_expert = 4 * SLOTS
    ours = ours_of(headers_of(near_ref, far_ref, width), x, tok, n_x)
    count = ours.shape[0]
    take = (iota((8, LANES), 1) == iota((8, LANES), 0) + HD).astype(BF16)
    line = dot(take, ours, ((1,), (1,)))
    ours = ours.astype(F32)
    lane = iota((count, LANES), 1)

    def column(i):
        return jnp.sum(jnp.where(lane == HD + i, ours, 0.0), axis=1, keepdims=True)

    first, second = iota((count, count), 0), iota((count, count), 1)
    before = (second < first) & (first // tok == second // tok)
    source = iota((count, rows), 1)
    group = iota((count, 1), 0) // tok
    pick = jnp.zeros((count, rows), F32)
    for k in range(TOPK):
        named = column(k)
        same = sum((line[m : m + 1, :] == named).astype(F32) for m in range(TOPK))
        slot = jnp.sum(jnp.where(before, same, 0.0), axis=1, keepdims=True).astype(jnp.int32)
        expert = named.astype(jnp.int32)
        place = (expert // 2) * per_expert + group * SLOTS + slot
        place = jnp.where(expert % 2 == c, place, -1)
        weight = sum(column(TOPK * (1 + i) + k) for i in range(3))
        pick = pick + jnp.where(source == place, weight, 0.0)
    high, low, _ = pieces(pick)
    returned = rows_ref[...]
    mixed = dot(high.astype(BF16), returned) + dot(low.astype(BF16), returned)
    kept_ref[...] = mixed[:pair]
    given_ref[...] = mixed[pair:].astype(BF16)


def join_cores(where_ref, kept_ref, got_ref, own_ref, given_ref):
    tok = own_ref.shape[0]
    own = where_ref[0]
    total = kept_ref[...] + got_ref[...].astype(F32)
    low, high = total[:tok], total[tok:]
    own_ref[...] = jnp.where(own == 0, low, high)
    given_ref[...] = jnp.where(own == 0, high, low).astype(BF16)


def finish(middle_ref, kept_ref, got_ref, gate_ref, out_ref):
    mixture = kept_ref[...] + got_ref[...].astype(F32)
    out_ref[...] = (middle_ref[...] + gate_ref[...] * mixture).astype(BF16)


def on_device(
    query_rows,
    key_rows,
    value_rows,
    residual,
    out_weight,
    attention_gate,
    norm_shift,
    norm_scale,
    expert_gate,
    expert_up,
    expert_down,
    routing,
    combine_weight,
):
    tok, width = query_rows.shape
    n_head = lax.axis_size(HEAD)
    n_x = lax.axis_size("x")
    n_z = lax.axis_size("z")
    n_plane = lax.axis_size(PLANE)
    cols = width // n_head
    rows = n_head * tok
    where = jnp.stack([lax.axis_index(a) for a in ("yh", "x", "c")]).astype(jnp.int32)
    gate, shift, scale = (a.reshape(1, width) for a in (attention_gate, norm_shift, norm_scale))

    own = local(
        prepare,
        shape((n_head, tok, 3 * cols + HD)),
        query_rows,
        key_rows,
        value_rows,
        routing.T,
        combine_weight.T,
        name="prepare",
    )
    own = exchange(own, HEAD).reshape(rows, 3 * cols + HD)
    near = gathered(own[:, cols + HD :], "yl").reshape(-1, 2 * cols)
    far = partner(near, "c")
    queries = gathered(own[:, :cols], "z").reshape(-1, cols)

    q_block = 256
    whole = pl.BlockSpec(near.shape, lambda i: (0, 0))
    packed = pl.pallas_call(
        attend,
        grid=(queries.shape[0] // q_block,),
        in_specs=[pl.BlockSpec((q_block, cols), lambda i: (i, 0)), whole, whole],
        out_specs=pl.BlockSpec((q_block, cols + HD), lambda i: (i, 0)),
        out_shape=shape((queries.shape[0], cols + HD)),
        name="attend",
    )(queries, near, far)
    packed = exchange(packed.reshape(n_z, rows, cols + HD), "z")

    partial = local(project, shape((n_x, 2 * tok, width)), packed, out_weight, name="project")
    gated, message = local(
        sum_pair,
        (shape((2 * tok, width), F32), shape((2 * tok, width))),
        where,
        exchange(partial, "x"),
        residual,
        gate,
        name="sum_pair",
        smem=(0,),
    )
    middle, near = local(
        normalize,
        (shape((tok, width), F32), shape((2 * tok, width + n_head // 2 * LANES))),
        where,
        gated,
        partner(message, "yh"),
        residual,
        shift,
        scale,
        own,
        name="normalize",
        smem=(0,),
    )
    far = partner(near, "c")

    buffer_rows = n_plane * 4 * SLOTS
    sent = local(
        lambda *refs: dispatch(*refs, width=width, n_x=n_x),
        shape((buffer_rows, width + LANES)),
        where,
        near,
        far,
        name="dispatch",
        smem=(0,),
    )
    arrived = exchange(sent.reshape(n_plane, -1, width + LANES), PLANE)
    arrived = arrived.reshape(buffer_rows, width + LANES)
    marks = arrived[:, width:].astype(F32)
    most = jnp.max(jnp.sum(marks[:, :n_x], axis=0)) / (4 * SLOTS)
    filled = marks[:, n_x]

    def expert(buffer):
        hidden = jax.nn.gelu(dot(buffer, expert_up[0]), approximate=True).astype(BF16)
        return dot(hidden, expert_down[0])

    def around(buffer):
        half = buffer.shape[0] // 2
        right = shifted(buffer, 1)
        left = shifted(buffer, -1)
        far_low = shifted(right[:half], 1)
        far_high = shifted(left[half:], -1)
        mine = expert(buffer)
        from_left = expert(right)
        from_right = expert(left)
        opposite = expert(jnp.concatenate([far_low, far_high], axis=0)).astype(BF16)
        low = shifted(opposite[:half], 1).astype(F32)
        high = shifted(opposite[half:], -1).astype(F32)
        to_right = jnp.concatenate([from_right[:half] + low, from_right[half:]], axis=0)
        to_left = jnp.concatenate([from_left[:half], from_left[half:] + high], axis=0)
        got = shifted(to_right.astype(BF16), 1).astype(F32)
        got = got + shifted(to_left.astype(BF16), -1).astype(F32)
        return (mine + got).astype(BF16)

    def many(operands):
        return around(operands[0])

    def few(operands):
        buffer, marked = operands
        at = jnp.arange(buffer_rows)
        upto = (at[None, :] < at[:, None]).astype(BF16)
        place = dot(upto, marked.astype(BF16)[:, None])[:, 0].astype(jnp.int32)
        place = jnp.where(marked > 0.5, place, -1)
        squeeze = (jnp.arange(FEW)[:, None] == place[None, :]).astype(BF16)
        results = around(dot(squeeze, buffer).astype(BF16))
        return dot(squeeze, results, ((0,), (0,))).astype(BF16)

    summed = lax.cond(most > FEW, many, few, (arrived[:, :width], filled))
    returned = exchange(summed.reshape(n_plane, -1, width), PLANE).reshape(buffer_rows, width)

    kept, given = local(
        lambda *refs: mix(*refs, width=width, n_x=n_x),
        (shape((2 * tok, width), F32), shape((2 * tok, width))),
        where,
        near,
        far,
        returned,
        name="mix",
        smem=(0,),
    )
    kept, given = local(
        join_cores,
        (shape((tok, width), F32), shape((tok, width))),
        where,
        kept,
        partner(given, "c"),
        name="join_cores",
        smem=(0,),
    )
    return local(
        finish,
        shape((tok, width)),
        middle,
        kept,
        partner(given, "yh"),
        expert_gate.reshape(1, width),
        name="finish",
    )


def solution(mesh):
    split = Mesh(mesh.devices.reshape(2, 4, 4, 8, 2), AXES)
    everywhere = P(AXES, None)
    placed = (
        everywhere,
        everywhere,
        everywhere,
        everywhere,
        P(HEAD, None),
        P(),
        P(),
        P(),
        P(),
        P(BLK, None, HEAD),
        P(BLK, HEAD, None),
        everywhere,
        everywhere,
    )
    return jax.shard_map(
        on_device, mesh=split, in_specs=placed, out_specs=everywhere, check_vma=False
    )
```

```python
import math

import jax
import jax.numpy as jnp
from jax import lax
from jax.experimental import pallas as pl
from jax.experimental.pallas import tpu as pltpu
from jax.sharding import Mesh
from jax.sharding import PartitionSpec as P

HD = 64
TOPK = 2
SLOTS = 2
FEW = 96
LANES = 128
AXES = ("yh", "x", "yl", "z", "c")
HEAD = ("yh", "x")
BLK = ("yl", "z", "c")
PLANE = ("yl", "z")
BF16 = jnp.bfloat16
F32 = jnp.float32
RATE = math.log2(math.e) / math.sqrt(HD)


def exchange(array, axis):
    return lax.all_to_all(array, axis, 0, 0, tiled=True)


def gathered(array, axis):
    copies = jnp.broadcast_to(array[None], (lax.axis_size(axis), *array.shape))
    return exchange(copies, axis)


def partner(array, axis):
    return lax.ppermute(array, axis, [(0, 1), (1, 0)])


def shifted(array, by, axis="x"):
    n = lax.axis_size(axis)
    return lax.ppermute(array, axis, [(i, (i + by) % n) for i in range(n)])


def iota(shape, dim):
    return lax.broadcasted_iota(jnp.int32, shape, dim)


def dot(a, b, dims=((1,), (0,))):
    return lax.dot_general(a, b, (dims, ((), ())), preferred_element_type=F32)


def pieces(values):
    out = []
    for _ in range(3):
        piece = values.astype(BF16).astype(F32)
        out.append(piece)
        values = values - piece
    return out


def local(body, outs, *args, name, smem=(), **kw):
    specs = [
        pl.BlockSpec(memory_space=pltpu.SMEM if i in smem else pltpu.VMEM)
        for i in range(len(args))
    ]
    return pl.pallas_call(
        body,
        out_shape=outs,
        in_specs=specs,
        out_specs=jax.tree.map(lambda _: pl.BlockSpec(memory_space=pltpu.VMEM), outs),
        name=name,
        **kw,
    )(*args)


def shape(dims, kind=BF16):
    return jax.ShapeDtypeStruct(dims, kind)


def prepare(q_ref, k_ref, v_ref, route_ref, weight_ref, out_ref):
    groups, tok, _ = out_ref.shape
    cols = q_ref.shape[1] // groups
    weight = weight_ref[...]
    lines = [route_ref[k : k + 1, :].astype(F32) for k in range(TOPK)]
    for piece in pieces(weight):
        lines += [piece[k : k + 1, :] for k in range(TOPK)]
    row = iota((16, tok), 0)
    table = jnp.zeros((16, tok), F32)
    for i, line in enumerate(lines):
        table = jnp.where(row == i, line, table)
    pick = (iota((16, HD), 0) == iota((16, HD), 1)).astype(BF16)
    header = dot(table.astype(BF16), pick, ((0,), (0,))).astype(BF16)
    for g in range(groups):
        span = slice(g * cols, (g + 1) * cols)
        out_ref[g] = jnp.concatenate(
            [q_ref[:, span], header, k_ref[:, span], v_ref[:, span]], axis=1
        )


def attend(q_ref, near_ref, far_ref, out_ref):
    rows, cols = q_ref.shape[0], q_ref.shape[1] - HD
    heads = cols // HD
    q = q_ref[:, :cols]
    near_k, far_k = near_ref[:, :cols], far_ref[:, :cols]
    near_v, far_v = near_ref[:, LANES:], far_ref[:, LANES:]
    q_head = iota((rows, cols), 1) // HD
    lane = iota((rows, cols + HD), 1)
    out = jnp.zeros((rows, cols + HD), F32)
    for j in range(heads):
        q_j = jnp.where(q_head == j, q, jnp.zeros_like(q))
        near = dot(q_j, near_k, ((1,), (1,)))
        far = dot(q_j, far_k, ((1,), (1,)))
        peak = jnp.maximum(
            jnp.max(near, axis=1, keepdims=True), jnp.max(far, axis=1, keepdims=True)
        )
        near = jnp.exp2((near - peak) * RATE)
        far = jnp.exp2((far - peak) * RATE)
        total = jnp.sum(near, axis=1, keepdims=True) + jnp.sum(far, axis=1, keepdims=True)
        accum = dot(near.astype(BF16), near_v) + dot(far.astype(BF16), far_v)
        out = jnp.where(lane // HD == j + 1, accum * (1.0 / total), out)
        for i, piece in enumerate(pieces(peak) + pieces(total)):
            out = jnp.where(lane == 6 * j + i, piece, out)
    out_ref[...] = out.astype(BF16)


def project(parts_ref, weight_ref, out_ref):
    count, rows, wide = parts_ref.shape
    n_x, pair_rows, _ = out_ref.shape
    tok = pair_rows // 2
    stats = parts_ref[:, :, :LANES].reshape(count * rows, LANES)
    src = iota((LANES, wide), 0)
    head = jnp.maximum(iota((LANES, wide), 1) // HD - 1, 0)
    at = src - 6 * head
    peak = dot(stats, ((at >= 0) & (at < 3)).astype(BF16)).reshape(count, rows, wide)
    total = dot(stats, ((at >= 3) & (at < 6)).astype(BF16)).reshape(count, rows, wide)
    top = jnp.max(peak, axis=0)
    share = total * jnp.exp2((peak - top[None]) * RATE)
    numer = jnp.sum(share * parts_ref[...].astype(F32), axis=0)
    attended = (numer / jnp.sum(share, axis=0))[:, HD:].astype(BF16)
    projected = dot(attended, weight_ref[...]).astype(BF16)
    for side in range(2):
        for x in range(n_x):
            start = (side * n_x + x) * tok
            out_ref[x, side * tok : (side + 1) * tok, :] = projected[start : start + tok]


def sum_pair(where_ref, parts_ref, residual_ref, gate_ref, sum_ref, out_ref):
    tok = residual_ref.shape[0]
    total = parts_ref[0].astype(F32)
    for x in range(1, parts_ref.shape[0]):
        total = total + parts_ref[x].astype(F32)
    total = total * gate_ref[...]
    sum_ref[...] = total
    own = where_ref[0]
    residual = residual_ref[...].astype(F32)
    for side in range(2):
        span = slice(side * tok, (side + 1) * tok)
        added = jnp.where(own == side, residual, 0.0)
        out_ref[span, :] = (total[span] + added).astype(BF16)


def normalize(
    where_ref, sum_ref, got_ref, residual_ref, shift_ref, scale_ref, own_ref, middle_ref, out_ref
):
    tok, width = residual_ref.shape
    own = where_ref[0]
    residual = residual_ref[...].astype(F32)
    for side in range(2):
        span = slice(side * tok, (side + 1) * tok)
        added = jnp.where(own == side, residual, 0.0)
        middle = sum_ref[span, :] + got_ref[span, :].astype(F32) + added

        @pl.when(own == side)
        def _():
            middle_ref[...] = middle

        average = jnp.mean(middle, axis=1, keepdims=True)
        centered = middle - average
        variance = jnp.mean(centered * centered, axis=1, keepdims=True)
        scaled = centered * lax.rsqrt(variance + 1e-06) * (1.0 + scale_ref[...])
        out_ref[span, :width] = (scaled + shift_ref[...]).astype(BF16)
    both = 2 * tok
    for i in range(own_ref.shape[0] // both):
        start = width + i * LANES
        out_ref[:, start : start + LANES] = own_ref[i * both : (i + 1) * both, LANES : 2 * LANES]


def headers_of(near_ref, far_ref, width):
    rows = []
    for ref in (near_ref, far_ref):
        for i in range((ref.shape[1] - width) // LANES):
            start = width + i * LANES
            rows.append(ref[:, start : start + LANES])
    return jnp.concatenate(rows, axis=0)


def ours_of(headers, x, tok, n_x):
    count = 4 * tok
    row, col = iota((count, headers.shape[0]), 0), iota((count, headers.shape[0]), 1)
    wanted = ((row // tok) * n_x + x) * tok + row % tok
    return dot((col == wanted).astype(BF16), headers).astype(BF16)


def dispatch(where_ref, near_ref, far_ref, out_ref, *, width, n_x):
    pair = near_ref.shape[0]
    tok = pair // 2
    x, c = where_ref[1], where_ref[2]
    rows = out_ref.shape[0]
    per_expert = 4 * SLOTS
    headers = headers_of(near_ref, far_ref, width)
    ours = ours_of(headers, x, tok, n_x)
    count = ours.shape[0]
    take = (iota((8, LANES), 1) == iota((8, LANES), 0) + HD).astype(BF16)
    line = dot(take, ours, ((1,), (1,)))
    col = [jnp.sum(jnp.where(iota((count, LANES), 1) == HD + k, ours.astype(F32), 0.0), axis=1, keepdims=True) for k in range(TOPK)]
    first, second = iota((count, count), 0), iota((count, count), 1)
    before = (first < second) & (first // tok == second // tok)
    hits = jnp.zeros((rows, count), F32)
    target = iota((rows, count), 0)
    group = iota((1, count), 1) // tok
    for k in range(TOPK):
        named = line[k : k + 1, :]
        same = sum((col[m] == named).astype(F32) for m in range(TOPK))
        slot = jnp.sum(jnp.where(before, same, 0.0), axis=0, keepdims=True).astype(jnp.int32)
        expert = named.astype(jnp.int32)
        place = (expert // 2) * per_expert + group * SLOTS + slot
        place = jnp.where(expert % 2 == c, place, -1)
        hits = hits + (target == place).astype(F32)
    onehot = hits.astype(BF16)
    out_ref[:, :width] = (
        dot(onehot[:, :pair], near_ref[:, :width]) + dot(onehot[:, pair:], far_ref[:, :width])
    ).astype(BF16)
    every = headers.shape[0]
    lines = dot(take, headers, ((1,), (1,)))
    named_here = (iota((rows, every), 0) // per_expert * 2 + c).astype(F32)
    named = sum((lines[k : k + 1, :] == named_here).astype(F32) for k in range(TOPK))
    member = (iota((every, LANES), 0) // tok % n_x == iota((every, LANES), 1)).astype(BF16)
    counts = dot(named.astype(BF16), member)
    filled = jnp.sum(hits, axis=1, keepdims=True)
    marks = jnp.where(iota((rows, LANES), 1) == n_x, filled, counts)
    out_ref[:, width:] = marks.astype(BF16)


def mix(where_ref, near_ref, far_ref, rows_ref, kept_ref, given_ref, *, width, n_x):
    pair = near_ref.shape[0]
    tok = pair // 2
    x, c = where_ref[1], where_ref[2]
    rows = rows_ref.shape[0]
    per_expert = 4 * SLOTS
    ours = ours_of(headers_of(near_ref, far_ref, width), x, tok, n_x)
    count = ours.shape[0]
    take = (iota((8, LANES), 1) == iota((8, LANES), 0) + HD).astype(BF16)
    line = dot(take, ours, ((1,), (1,)))
    ours = ours.astype(F32)
    lane = iota((count, LANES), 1)

    def column(i):
        return jnp.sum(jnp.where(lane == HD + i, ours, 0.0), axis=1, keepdims=True)

    first, second = iota((count, count), 0), iota((count, count), 1)
    before = (second < first) & (first // tok == second // tok)
    source = iota((count, rows), 1)
    group = iota((count, 1), 0) // tok
    pick = jnp.zeros((count, rows), F32)
    for k in range(TOPK):
        named = column(k)
        same = sum((line[m : m + 1, :] == named).astype(F32) for m in range(TOPK))
        slot = jnp.sum(jnp.where(before, same, 0.0), axis=1, keepdims=True).astype(jnp.int32)
        expert = named.astype(jnp.int32)
        place = (expert // 2) * per_expert + group * SLOTS + slot
        place = jnp.where(expert % 2 == c, place, -1)
        weight = sum(column(TOPK * (1 + i) + k) for i in range(3))
        pick = pick + jnp.where(source == place, weight, 0.0)
    high, low, _ = pieces(pick)
    returned = rows_ref[...]
    mixed = dot(high.astype(BF16), returned) + dot(low.astype(BF16), returned)
    kept_ref[...] = mixed[:pair]
    given_ref[...] = mixed[pair:].astype(BF16)


def join_cores(where_ref, kept_ref, got_ref, own_ref, given_ref):
    tok = own_ref.shape[0]
    own = where_ref[0]
    total = kept_ref[...] + got_ref[...].astype(F32)
    low, high = total[:tok], total[tok:]
    own_ref[...] = jnp.where(own == 0, low, high)
    given_ref[...] = jnp.where(own == 0, high, low).astype(BF16)


def finish(middle_ref, kept_ref, got_ref, gate_ref, out_ref):
    mixture = kept_ref[...] + got_ref[...].astype(F32)
    out_ref[...] = (middle_ref[...] + gate_ref[...] * mixture).astype(BF16)


def on_device(
    query_rows,
    key_rows,
    value_rows,
    residual,
    out_weight,
    attention_gate,
    norm_shift,
    norm_scale,
    expert_gate,
    expert_up,
    expert_down,
    routing,
    combine_weight,
):
    tok, width = query_rows.shape
    n_head = lax.axis_size(HEAD)
    n_x = lax.axis_size("x")
    n_z = lax.axis_size("z")
    n_plane = lax.axis_size(PLANE)
    cols = width // n_head
    rows = n_head * tok
    where = jnp.stack([lax.axis_index(a) for a in ("yh", "x", "c")]).astype(jnp.int32)
    gate, shift, scale = (a.reshape(1, width) for a in (attention_gate, norm_shift, norm_scale))

    own = local(
        prepare,
        shape((n_head, tok, 3 * cols + HD)),
        query_rows,
        key_rows,
        value_rows,
        routing.T,
        combine_weight.T,
        name="prepare",
    )
    own = exchange(own, HEAD).reshape(rows, 3 * cols + HD)
    near = own[:, cols + HD :]
    near = jnp.concatenate([near] + [shifted(near, turn, "yl") for turn in (1, 2, 3)], axis=0)
    far = partner(near, "c")
    queries = gathered(own[:, : cols + HD], "z").reshape(-1, cols + HD)

    q_block = 256
    whole = pl.BlockSpec(near.shape, lambda i: (0, 0))
    packed = pl.pallas_call(
        attend,
        grid=(queries.shape[0] // q_block,),
        in_specs=[pl.BlockSpec((q_block, cols + HD), lambda i: (i, 0)), whole, whole],
        out_specs=pl.BlockSpec((q_block, cols + HD), lambda i: (i, 0)),
        out_shape=shape((queries.shape[0], cols + HD)),
        name="attend",
    )(queries, near, far)
    packed = exchange(packed.reshape(n_z, rows, cols + HD), "z")

    partial = local(project, shape((n_x, 2 * tok, width)), packed, out_weight, name="project")
    gated, message = local(
        sum_pair,
        (shape((2 * tok, width), F32), shape((2 * tok, width))),
        where,
        exchange(partial, "x"),
        residual,
        gate,
        name="sum_pair",
        smem=(0,),
    )
    middle, near = local(
        normalize,
        (shape((tok, width), F32), shape((2 * tok, width + n_head // 2 * LANES))),
        where,
        gated,
        partner(message, "yh"),
        residual,
        shift,
        scale,
        own,
        name="normalize",
        smem=(0,),
    )
    far = partner(near, "c")

    buffer_rows = n_plane * 4 * SLOTS
    sent = local(
        lambda *refs: dispatch(*refs, width=width, n_x=n_x),
        shape((buffer_rows, width + LANES)),
        where,
        near,
        far,
        name="dispatch",
        smem=(0,),
    )
    arrived = exchange(sent.reshape(n_plane, -1, width + LANES), PLANE)
    arrived = arrived.reshape(buffer_rows, width + LANES)
    marks = arrived[:, width:].astype(F32)
    most = jnp.max(jnp.sum(marks[:, :n_x], axis=0)) / (4 * SLOTS)
    filled = marks[:, n_x]

    def expert(buffer):
        hidden = jax.nn.gelu(dot(buffer, expert_up[0]), approximate=True).astype(BF16)
        return dot(hidden, expert_down[0])

    def around(buffer):
        n_ring = lax.axis_size("x")
        turns = range(1, n_ring)
        others = [shifted(buffer, turn) for turn in turns]
        total = expert(buffer)
        results = [expert(other).astype(BF16) for other in others]
        for turn, result in zip(turns, results):
            total = total + shifted(result, -turn).astype(F32)
        return total.astype(BF16)

    def many(operands):
        return around(operands[0])

    def few(operands):
        buffer, marked = operands
        at = jnp.arange(buffer_rows)
        upto = (at[None, :] < at[:, None]).astype(BF16)
        place = dot(upto, marked.astype(BF16)[:, None])[:, 0].astype(jnp.int32)
        place = jnp.where(marked > 0.5, place, -1)
        squeeze = (jnp.arange(FEW)[:, None] == place[None, :]).astype(BF16)
        results = around(dot(squeeze, buffer).astype(BF16))
        return dot(squeeze, results, ((0,), (0,))).astype(BF16)

    summed = lax.cond(most > FEW, many, few, (arrived[:, :width], filled))
    returned = exchange(summed.reshape(n_plane, -1, width), PLANE).reshape(buffer_rows, width)

    kept, given = local(
        lambda *refs: mix(*refs, width=width, n_x=n_x),
        (shape((2 * tok, width), F32), shape((2 * tok, width))),
        where,
        near,
        far,
        returned,
        name="mix",
        smem=(0,),
    )
    kept, given = local(
        join_cores,
        (shape((tok, width), F32), shape((tok, width))),
        where,
        kept,
        partner(given, "c"),
        name="join_cores",
        smem=(0,),
    )
    return local(
        finish,
        shape((tok, width)),
        middle,
        kept,
        partner(given, "yh"),
        expert_gate.reshape(1, width),
        name="finish",
    )


def solution(mesh):
    split = Mesh(mesh.devices.reshape(2, 4, 4, 8, 2), AXES)
    everywhere = P(AXES, None)
    placed = (
        everywhere,
        everywhere,
        everywhere,
        everywhere,
        P(HEAD, None),
        P(),
        P(),
        P(),
        P(),
        P(BLK, None, HEAD),
        P(BLK, HEAD, None),
        everywhere,
        everywhere,
    )
    return jax.shard_map(
        on_device, mesh=split, in_specs=placed, out_specs=everywhere, check_vma=False
    )
```

```python
import math

import jax
import jax.numpy as jnp
from jax import lax
from jax.experimental import pallas as pl
from jax.experimental.pallas import tpu as pltpu
from jax.sharding import Mesh
from jax.sharding import PartitionSpec as P

HD = 64
TOPK = 2
SLOTS = 2
LANES = 128
AXES = ("yh", "x", "yl", "z", "c")
HEAD = ("yh", "x")
BLK = ("yl", "z", "c")
PLANE = ("yl", "z")
BF16 = jnp.bfloat16
F32 = jnp.float32
RATE = math.log2(math.e) / math.sqrt(HD)


def exchange(array, axis):
    return lax.all_to_all(array, axis, 0, 0, tiled=True)


def gathered(array, axis):
    copies = jnp.broadcast_to(array[None], (lax.axis_size(axis), *array.shape))
    return exchange(copies, axis)


def partner(array, axis):
    return lax.ppermute(array, axis, [(0, 1), (1, 0)])


def shifted(array, by, axis="x"):
    n = lax.axis_size(axis)
    return lax.ppermute(array, axis, [(i, (i + by) % n) for i in range(n)])


def iota(shape, dim):
    return lax.broadcasted_iota(jnp.int32, shape, dim)


def dot(a, b, dims=((1,), (0,))):
    return lax.dot_general(a, b, (dims, ((), ())), preferred_element_type=F32)


def pieces(values):
    out = []
    for _ in range(3):
        piece = values.astype(BF16).astype(F32)
        out.append(piece)
        values = values - piece
    return out


def local(body, outs, *args, smem=(), **kw):
    specs = [
        pl.BlockSpec(memory_space=pltpu.SMEM if i in smem else pltpu.VMEM)
        for i in range(len(args))
    ]
    return pl.pallas_call(
        body,
        out_shape=outs,
        in_specs=specs,
        out_specs=jax.tree.map(lambda _: pl.BlockSpec(memory_space=pltpu.VMEM), outs),
        **kw,
    )(*args)


def shape(dims, kind=BF16):
    return jax.ShapeDtypeStruct(dims, kind)


def prepare(q_ref, k_ref, v_ref, route_ref, weight_ref, out_ref):
    groups, tok, _ = out_ref.shape
    cols = q_ref.shape[1] // groups
    weight = weight_ref[...]
    lines = [route_ref[k : k + 1, :].astype(F32) for k in range(TOPK)]
    for piece in pieces(weight):
        lines += [piece[k : k + 1, :] for k in range(TOPK)]
    row = iota((16, tok), 0)
    table = jnp.zeros((16, tok), F32)
    for i, line in enumerate(lines):
        table = jnp.where(row == i, line, table)
    pick = (iota((16, HD), 0) == iota((16, HD), 1)).astype(BF16)
    header = dot(table.astype(BF16), pick, ((0,), (0,))).astype(BF16)
    for g in range(groups):
        span = slice(g * cols, (g + 1) * cols)
        out_ref[g] = jnp.concatenate(
            [q_ref[:, span], header, k_ref[:, span], v_ref[:, span]], axis=1
        )


def attend(q_ref, near_ref, far_ref, out_ref):
    rows, cols = q_ref.shape[0], q_ref.shape[1] - HD
    heads = cols // HD
    q = q_ref[:, :cols]
    near_k, far_k = near_ref[:, :cols], far_ref[:, :cols]
    near_v, far_v = near_ref[:, LANES:], far_ref[:, LANES:]
    q_head = iota((rows, cols), 1) // HD
    lane = iota((rows, cols + HD), 1)
    out = jnp.zeros((rows, cols + HD), F32)
    for j in range(heads):
        q_j = jnp.where(q_head == j, q, jnp.zeros_like(q))
        near = dot(q_j, near_k, ((1,), (1,)))
        far = dot(q_j, far_k, ((1,), (1,)))
        peak = jnp.maximum(
            jnp.max(near, axis=1, keepdims=True), jnp.max(far, axis=1, keepdims=True)
        )
        near = jnp.exp2((near - peak) * RATE)
        far = jnp.exp2((far - peak) * RATE)
        total = jnp.sum(near, axis=1, keepdims=True) + jnp.sum(far, axis=1, keepdims=True)
        accum = dot(near.astype(BF16), near_v) + dot(far.astype(BF16), far_v)
        out = jnp.where(lane // HD == j + 1, accum * (1.0 / total), out)
        for i, piece in enumerate(pieces(peak) + pieces(total)):
            out = jnp.where(lane == 6 * j + i, piece, out)
    out_ref[...] = out.astype(BF16)


def project(parts_ref, weight_ref, out_ref):
    count, rows, wide = parts_ref.shape
    n_x, pair_rows, _ = out_ref.shape
    tok = pair_rows // 2
    stats = parts_ref[:, :, :LANES].reshape(count * rows, LANES)
    src = iota((LANES, wide), 0)
    head = jnp.maximum(iota((LANES, wide), 1) // HD - 1, 0)
    at = src - 6 * head
    peak = dot(stats, ((at >= 0) & (at < 3)).astype(BF16)).reshape(count, rows, wide)
    total = dot(stats, ((at >= 3) & (at < 6)).astype(BF16)).reshape(count, rows, wide)
    top = jnp.max(peak, axis=0)
    share = total * jnp.exp2((peak - top[None]) * RATE)
    numer = jnp.sum(share * parts_ref[...].astype(F32), axis=0)
    attended = (numer / jnp.sum(share, axis=0))[:, HD:].astype(BF16)
    projected = dot(attended, weight_ref[...]).astype(BF16)
    for side in range(2):
        for x in range(n_x):
            start = (side * n_x + x) * tok
            out_ref[x, side * tok : (side + 1) * tok, :] = projected[start : start + tok]


def normalize(
    where_ref, sum_ref, got_ref, residual_ref, shift_ref, factor_ref, own_ref, middle_ref, out_ref
):
    tok, width = residual_ref.shape
    own, x, n_x = where_ref[0], where_ref[1], own_ref.shape[0] // (2 * tok)
    residual = residual_ref[...].astype(F32)
    for side in range(2):
        span = slice(side * tok, (side + 1) * tok)
        added = jnp.where(own == side, residual, 0.0)
        middle = sum_ref[span, :] + got_ref[span, :].astype(F32) + added

        @pl.when(own == side)
        def _():
            middle_ref[...] = middle

        average = jnp.mean(middle, axis=1, keepdims=True)
        centered = middle - average
        variance = jnp.mean(centered * centered, axis=1, keepdims=True)
        scaled = centered * lax.rsqrt(variance + 1e-06) * factor_ref[...]
        out_ref[span, :width] = (scaled + shift_ref[...]).astype(BF16)
        start = pl.multiple_of((side * n_x + x) * tok, tok)
        out_ref[span, width:] = own_ref[pl.ds(start, tok), LANES : 2 * LANES]


def places(near_ref, far_ref, c, width, across):
    pair = near_ref.shape[0]
    tok = pair // 2
    count = 2 * pair
    headers = jnp.concatenate([near_ref[:, width:], far_ref[:, width:]], axis=0)
    take = (iota((8, LANES), 1) == iota((8, LANES), 0) + HD).astype(BF16)
    lines = dot(take, headers, ((1,), (1,)))
    headers = headers.astype(F32)
    lane = iota((count, LANES), 1)

    def column(i):
        return jnp.sum(jnp.where(lane == HD + i, headers, 0.0), axis=1, keepdims=True)

    line = [lines[k : k + 1, :] for k in range(TOPK)]
    col = [column(k) for k in range(TOPK)]
    named, others, axis = (line, col, 0) if across else (col, line, 1)
    this, other = iota((count, count), 1 - axis), iota((count, count), axis)
    before = (other < this) & (this // tok == other // tok)
    group = iota((1, count), 1) // tok if across else iota((count, 1), 0) // tok
    out = []
    for k in range(TOPK):
        same = sum((other_k == named[k]).astype(F32) for other_k in others)
        slot = jnp.sum(jnp.where(before, same, 0.0), axis=axis, keepdims=True).astype(jnp.int32)
        expert = named[k].astype(jnp.int32)
        place = (expert // 2) * (4 * SLOTS) + group * SLOTS + slot
        out.append(jnp.where(expert % 2 == c, place, -1))
    return out, column


def dispatch(where_ref, near_ref, far_ref, out_ref):
    rows, width = out_ref.shape
    pair = near_ref.shape[0]
    chosen, _ = places(near_ref, far_ref, where_ref[2], width, True)
    target = iota((rows, 2 * pair), 0)
    onehot = sum((target == place).astype(F32) for place in chosen).astype(BF16)
    out_ref[...] = (
        dot(onehot[:, :pair], near_ref[:, :width]) + dot(onehot[:, pair:], far_ref[:, :width])
    ).astype(BF16)


def run_expert(rows_ref, *refs):
    *weights, out_ref, up_buf, down_buf, sem = refs
    count = len(weights) // 2
    ups, downs = weights[:count], weights[count:]
    copies = []
    for i in range(count):
        copies.append(
            (
                pltpu.make_async_copy(ups[i], up_buf.at[i], sem.at[0, i]),
                pltpu.make_async_copy(downs[i], down_buf.at[i], sem.at[1, i]),
            )
        )
        for copy in copies[-1]:
            copy.start()
    rows = rows_ref[...]
    total = jnp.zeros(out_ref.shape, F32)
    for i in range(count):
        copies[i][0].wait()
        hidden = jax.nn.gelu(dot(rows, up_buf[i]), approximate=True).astype(BF16)
        copies[i][1].wait()
        total = total + dot(hidden, down_buf[i])
    out_ref[...] = total.astype(BF16)


def mix(where_ref, near_ref, far_ref, rows_ref, kept_ref, given_ref):
    rows, width = rows_ref.shape
    pair = near_ref.shape[0]
    chosen, column = places(near_ref, far_ref, where_ref[2], width, False)
    source = iota((2 * pair, rows), 1)
    pick = jnp.zeros((2 * pair, rows), F32)
    for k, place in enumerate(chosen):
        weight = sum(column(TOPK * (1 + i) + k) for i in range(3))
        pick = pick + jnp.where(source == place, weight, 0.0)
    high, low, _ = pieces(pick)
    returned = rows_ref[...]
    mixed = dot(high.astype(BF16), returned) + dot(low.astype(BF16), returned)
    kept_ref[...] = mixed[:pair]
    given_ref[...] = mixed[pair:].astype(BF16)


def layer(
    query_rows,
    key_rows,
    value_rows,
    residual,
    out_weight,
    attention_gate,
    norm_shift,
    norm_scale,
    expert_gate,
    expert_up,
    expert_down,
    routing,
    combine_weight,
):
    tok, width = query_rows.shape
    n_head = lax.axis_size(HEAD)
    n_x = lax.axis_size("x")
    n_z = lax.axis_size("z")
    n_plane = lax.axis_size(PLANE)
    cols = width // n_head
    rows = n_head * tok
    where = jnp.stack([lax.axis_index(a) for a in ("yh", "x", "c")]).astype(jnp.int32)
    factor = (1.0 + norm_scale).reshape(1, width)
    gate, shift = (a.reshape(1, width) for a in (attention_gate, norm_shift))

    own = local(
        prepare,
        shape((n_head, tok, 3 * cols + HD)),
        query_rows,
        key_rows,
        value_rows,
        routing.T,
        combine_weight.T,
    )
    own = exchange(own, HEAD).reshape(rows, 3 * cols + HD)

    up, down = expert_up[0], expert_down[0]
    up_left, up_right = shifted(up, 1), shifted(up, -1)
    down_left, down_right = shifted(down, 1), shifted(down, -1)
    up_far, down_far = shifted(up_left, 1), shifted(down_right, -1)
    near = own[:, cols + HD :]
    near = jnp.concatenate([near] + [shifted(near, turn, "yl") for turn in (1, 2, 3)], axis=0)
    far = partner(near, "c")
    queries = gathered(own[:, : cols + HD], "z").reshape(-1, cols + HD)

    q_block = 256
    whole = pl.BlockSpec(near.shape, lambda i: (0, 0))
    packed = pl.pallas_call(
        attend,
        grid=(queries.shape[0] // q_block,),
        in_specs=[pl.BlockSpec((q_block, cols + HD), lambda i: (i, 0)), whole, whole],
        out_specs=pl.BlockSpec((q_block, cols + HD), lambda i: (i, 0)),
        out_shape=shape((queries.shape[0], cols + HD)),
        name="attend",
    )(queries, near, far)
    packed = exchange(packed.reshape(n_z, rows, cols + HD), "z")

    partial = local(project, shape((n_x, 2 * tok, width)), packed, out_weight)
    parts = exchange(partial, "x")
    gated = jnp.sum(parts.astype(F32), axis=0) * gate
    first = where[0] == 0
    ours = jnp.where(first, gated[:tok], gated[tok:]) + residual.astype(F32)
    message = jnp.concatenate(
        [jnp.where(first, ours, gated[:tok]), jnp.where(first, gated[tok:], ours)], axis=0
    ).astype(BF16)
    middle, near = local(
        normalize,
        (shape((tok, width), F32), shape((2 * tok, width + LANES))),
        where,
        gated,
        partner(message, "yh"),
        residual,
        shift,
        factor,
        own,
        smem=(0,),
    )
    far = partner(near, "c")

    buffer_rows = n_plane * 4 * SLOTS
    sent = local(dispatch, shape((buffer_rows, width)), where, near, far, smem=(0,))
    arrived = exchange(sent.reshape(n_plane, -1, width), PLANE).reshape(buffer_rows, width)
    ups, downs = (up, up_left, up_right, up_far), (down, down_left, down_right, down_far)
    in_place = pl.BlockSpec(memory_space=pl.ANY)
    output = pl.pallas_call(
        run_expert,
        in_specs=[pl.BlockSpec(memory_space=pltpu.VMEM)] + [in_place] * (2 * n_x),
        out_specs=pl.BlockSpec(memory_space=pltpu.VMEM),
        out_shape=shape((buffer_rows, width)),
        scratch_shapes=[
            pltpu.VMEM((n_x, *up.shape), BF16),
            pltpu.VMEM((n_x, *down.shape), BF16),
            pltpu.SemaphoreType.DMA((2, n_x)),
        ],
        name="run_expert",
    )(arrived, *ups, *downs)
    returned = exchange(output.reshape(n_plane, -1, width), PLANE).reshape(buffer_rows, width)

    kept, given = local(
        mix,
        (shape((2 * tok, width), F32), shape((2 * tok, width))),
        where,
        near,
        far,
        returned,
        smem=(0,),
    )
    both = kept + partner(given, "c").astype(F32)
    low, high = both[:tok], both[tok:]
    given = jnp.where(first, high, low).astype(BF16)
    mixture = jnp.where(first, low, high) + partner(given, "yh").astype(F32)
    return (middle + expert_gate * mixture).astype(BF16)


def solution(mesh):
    split = Mesh(mesh.devices.reshape(2, 4, 4, 8, 2), AXES)
    everywhere = P(AXES, None)
    placed = (
        everywhere,
        everywhere,
        everywhere,
        everywhere,
        P(HEAD, None),
        P(),
        P(),
        P(),
        P(),
        P(BLK, None, HEAD),
        P(BLK, HEAD, None),
        everywhere,
        everywhere,
    )
    return jax.shard_map(layer, mesh=split, in_specs=placed, out_specs=everywhere, check_vma=False)
```

```python
import math

import jax
import jax.numpy as jnp
from jax import lax
from jax.experimental import pallas as pl
from jax.experimental.pallas import tpu as pltpu
from jax.sharding import Mesh
from jax.sharding import PartitionSpec as P

HD = 64
TOPK = 2
SLOTS = 2
LANES = 128
AXES = ("yh", "x", "yl", "z", "c")
HEAD = ("yh", "x")
BLK = ("yl", "z", "c")
PLANE = ("yl", "z")
BF16 = jnp.bfloat16
F32 = jnp.float32
RATE = math.log2(math.e) / math.sqrt(HD)


def exchange(array, axis):
    return lax.all_to_all(array, axis, 0, 0, tiled=True)


def gathered(array, axis):
    copies = jnp.broadcast_to(array[None], (lax.axis_size(axis), *array.shape))
    return exchange(copies, axis)


def partner(array, axis):
    return lax.ppermute(array, axis, [(0, 1), (1, 0)])


def shifted(array, by, axis="x"):
    n = lax.axis_size(axis)
    return lax.ppermute(array, axis, [(i, (i + by) % n) for i in range(n)])


def iota(shape, dim):
    return lax.broadcasted_iota(jnp.int32, shape, dim)


def dot(a, b, dims=((1,), (0,))):
    return lax.dot_general(a, b, (dims, ((), ())), preferred_element_type=F32)


def pieces(values):
    out = []
    for _ in range(3):
        piece = values.astype(BF16).astype(F32)
        out.append(piece)
        values = values - piece
    return out


def local(body, outs, *args, smem=(), elsewhere=(), **kw):
    specs, placed = [], []
    for i, arg in enumerate(args):
        if i in smem:
            specs.append(pl.BlockSpec(memory_space=pltpu.SMEM))
        elif i in elsewhere:
            specs.append(pl.BlockSpec(memory_space=pl.ANY))
        else:
            specs.append(pl.BlockSpec(memory_space=pltpu.VMEM))
            arg = pltpu.with_memory_space_constraint(arg, pltpu.VMEM)
        placed.append(arg)
    return pl.pallas_call(
        body,
        out_shape=jax.tree.map(lambda o: pltpu.VMEM(o.shape, o.dtype), outs),
        in_specs=specs,
        out_specs=jax.tree.map(lambda _: pl.BlockSpec(memory_space=pltpu.VMEM), outs),
        **kw,
    )(*placed)


def shape(dims, kind=BF16):
    return jax.ShapeDtypeStruct(dims, kind)


def prepare(q_ref, k_ref, v_ref, route_ref, weight_ref, out_ref):
    groups, tok, _ = out_ref.shape
    cols = q_ref.shape[1] // groups
    weight = weight_ref[...]
    lines = [route_ref[k : k + 1, :].astype(F32) for k in range(TOPK)]
    for piece in pieces(weight):
        lines += [piece[k : k + 1, :] for k in range(TOPK)]
    row = iota((16, tok), 0)
    table = jnp.zeros((16, tok), F32)
    for i, line in enumerate(lines):
        table = jnp.where(row == i, line, table)
    pick = (iota((16, HD), 0) == iota((16, HD), 1)).astype(BF16)
    header = dot(table.astype(BF16), pick, ((0,), (0,))).astype(BF16)
    for g in range(groups):
        span = slice(g * cols, (g + 1) * cols)
        out_ref[g] = jnp.concatenate(
            [q_ref[:, span], header, k_ref[:, span], v_ref[:, span]], axis=1
        )


def attend(q_ref, near_ref, far_ref, out_ref):
    wide = q_ref.shape[1]
    cols, rows = wide - HD, 256
    near_k, far_k = near_ref[:, :cols], far_ref[:, :cols]
    near_v, far_v = near_ref[:, LANES:], far_ref[:, LANES:]
    q_head = iota((rows, cols), 1) // HD
    o_head = iota((rows, wide), 1) // HD - 1
    lane = iota((rows, LANES), 1)
    for start in range(0, q_ref.shape[0], rows):
        q = q_ref[start : start + rows, :cols]
        out = jnp.zeros((rows, wide), F32)
        stats = jnp.zeros((rows, LANES), F32)
        for j in range(cols // HD):
            q_j = jnp.where(q_head == j, q, jnp.zeros_like(q))
            near = dot(q_j, near_k, ((1,), (1,)))
            far = dot(q_j, far_k, ((1,), (1,)))
            peak = jnp.maximum(
                jnp.max(near, axis=1, keepdims=True), jnp.max(far, axis=1, keepdims=True)
            )
            near = jnp.exp2((near - peak) * RATE)
            far = jnp.exp2((far - peak) * RATE)
            total = jnp.sum(near, axis=1, keepdims=True) + jnp.sum(far, axis=1, keepdims=True)
            accum = dot(near.astype(BF16), near_v) + dot(far.astype(BF16), far_v)
            out = jnp.where(o_head == j, accum * (1.0 / total), out)
            for i, piece in enumerate(pieces(peak) + pieces(total)):
                stats = jnp.where(lane == 6 * j + i, piece, stats)
        stats = jnp.where(lane < HD, stats, out[:, :LANES])
        out_ref[start : start + rows, :LANES] = stats.astype(BF16)
        out_ref[start : start + rows, LANES:] = out[:, LANES:].astype(BF16)


def project(parts_ref, weight_ref, out_ref):
    count, rows, wide = parts_ref.shape
    n_x, pair_rows, _ = out_ref.shape
    tok = pair_rows // 2
    stats = parts_ref[:, :, :LANES].reshape(count * rows, LANES)
    src = iota((LANES, wide), 0)
    head = jnp.maximum(iota((LANES, wide), 1) // HD - 1, 0)
    at = src - 6 * head
    peak = dot(stats, ((at >= 0) & (at < 3)).astype(BF16)).reshape(count, rows, wide)
    total = dot(stats, ((at >= 3) & (at < 6)).astype(BF16)).reshape(count, rows, wide)
    top = jnp.max(peak, axis=0)
    share = total * jnp.exp2((peak - top[None]) * RATE)
    numer = jnp.sum(share * parts_ref[...].astype(F32), axis=0)
    attended = (numer / jnp.sum(share, axis=0))[:, HD:].astype(BF16)
    projected = dot(attended, weight_ref[...]).astype(BF16)
    for side in range(2):
        for x in range(n_x):
            start = (side * n_x + x) * tok
            out_ref[x, side * tok : (side + 1) * tok, :] = projected[start : start + tok]


def normalize(
    where_ref, sum_ref, got_ref, residual_ref, shift_ref, factor_ref, own_ref, middle_ref, out_ref
):
    tok, width = residual_ref.shape
    own, x, n_x = where_ref[0], where_ref[1], own_ref.shape[0] // (2 * tok)
    residual = residual_ref[...].astype(F32)
    for side in range(2):
        span = slice(side * tok, (side + 1) * tok)
        added = jnp.where(own == side, residual, 0.0)
        middle = sum_ref[span, :] + got_ref[span, :].astype(F32) + added

        @pl.when(own == side)
        def _():
            middle_ref[...] = middle

        average = jnp.mean(middle, axis=1, keepdims=True)
        centered = middle - average
        variance = jnp.mean(centered * centered, axis=1, keepdims=True)
        scaled = centered * lax.rsqrt(variance + 1e-06) * factor_ref[...]
        out_ref[span, :width] = (scaled + shift_ref[...]).astype(BF16)
        start = pl.multiple_of((side * n_x + x) * tok, tok)
        out_ref[span, width:] = own_ref[pl.ds(start, tok), LANES : 2 * LANES]


def places(near_ref, far_ref, c, width, across):
    pair = near_ref.shape[0]
    tok = pair // 2
    count = 2 * pair
    headers = jnp.concatenate([near_ref[:, width:], far_ref[:, width:]], axis=0)
    take = (iota((8, LANES), 1) == iota((8, LANES), 0) + HD).astype(BF16)
    lines = dot(take, headers, ((1,), (1,)))
    headers = headers.astype(F32)
    lane = iota((count, LANES), 1)

    def column(i):
        return jnp.sum(jnp.where(lane == HD + i, headers, 0.0), axis=1, keepdims=True)

    line = [lines[k : k + 1, :] for k in range(TOPK)]
    col = [column(k) for k in range(TOPK)]
    named, others, axis = (line, col, 0) if across else (col, line, 1)
    this, other = iota((count, count), 1 - axis), iota((count, count), axis)
    before = (other < this) & (this // tok == other // tok)
    group = iota((1, count), 1) // tok if across else iota((count, 1), 0) // tok
    out = []
    for k in range(TOPK):
        same = sum((other_k == named[k]).astype(F32) for other_k in others)
        slot = jnp.sum(jnp.where(before, same, 0.0), axis=axis, keepdims=True).astype(jnp.int32)
        expert = named[k].astype(jnp.int32)
        place = (expert // 2) * (4 * SLOTS) + group * SLOTS + slot
        out.append(jnp.where(expert % 2 == c, place, -1))
    return out, column


def dispatch(where_ref, near_ref, far_ref, out_ref):
    rows, width = out_ref.shape
    pair = near_ref.shape[0]
    chosen, _ = places(near_ref, far_ref, where_ref[2], width, True)
    target = iota((rows, 2 * pair), 0)
    onehot = sum((target == place).astype(F32) for place in chosen).astype(BF16)
    out_ref[...] = (
        dot(onehot[:, :pair], near_ref[:, :width]) + dot(onehot[:, pair:], far_ref[:, :width])
    ).astype(BF16)


def run_expert(rows_ref, *refs):
    *weights, out_ref, up_buf, down_buf, sem = refs
    count = len(weights) // 2
    ups, downs = weights[:count], weights[count:]
    copies = []
    for i in range(count):
        copies.append(
            (
                pltpu.make_async_copy(ups[i], up_buf.at[i], sem.at[0, i]),
                pltpu.make_async_copy(downs[i], down_buf.at[i], sem.at[1, i]),
            )
        )
        for copy in copies[-1]:
            copy.start()
    rows = rows_ref[...]
    total = jnp.zeros(out_ref.shape, F32)
    for i in range(count):
        copies[i][0].wait()
        hidden = jax.nn.gelu(dot(rows, up_buf[i]), approximate=True).astype(BF16)
        copies[i][1].wait()
        total = total + dot(hidden, down_buf[i])
    out_ref[...] = total.astype(BF16)


def mix(where_ref, near_ref, far_ref, rows_ref, kept_ref, given_ref):
    rows, width = rows_ref.shape
    pair = near_ref.shape[0]
    chosen, column = places(near_ref, far_ref, where_ref[2], width, False)
    source = iota((2 * pair, rows), 1)
    pick = jnp.zeros((2 * pair, rows), F32)
    for k, place in enumerate(chosen):
        weight = sum(column(TOPK * (1 + i) + k) for i in range(3))
        pick = pick + jnp.where(source == place, weight, 0.0)
    high, low, _ = pieces(pick)
    returned = rows_ref[...]
    mixed = dot(high.astype(BF16), returned) + dot(low.astype(BF16), returned)
    kept_ref[...] = mixed[:pair]
    given_ref[...] = mixed[pair:].astype(BF16)


def layer(
    query_rows,
    key_rows,
    value_rows,
    residual,
    out_weight,
    attention_gate,
    norm_shift,
    norm_scale,
    expert_gate,
    expert_up,
    expert_down,
    routing,
    combine_weight,
):
    tok, width = query_rows.shape
    n_head = lax.axis_size(HEAD)
    n_x = lax.axis_size("x")
    n_z = lax.axis_size("z")
    n_plane = lax.axis_size(PLANE)
    cols = width // n_head
    rows = n_head * tok
    where = jnp.stack([lax.axis_index(a) for a in ("yh", "x", "c")]).astype(jnp.int32)
    factor = (1.0 + norm_scale).reshape(1, width)
    gate, shift = (a.reshape(1, width) for a in (attention_gate, norm_shift))

    own = pl.pallas_call(
        prepare, out_shape=pltpu.VMEM((n_head, tok, 3 * cols + HD), BF16), name="prepare"
    )(query_rows, key_rows, value_rows, routing.T, combine_weight.T)
    own = exchange(own, HEAD).reshape(rows, 3 * cols + HD)

    up, down = expert_up[0], expert_down[0]
    up_left, up_right = shifted(up, 1), shifted(up, -1)
    down_left, down_right = shifted(down, 1), shifted(down, -1)
    up_far, down_far = shifted(up_left, 1), shifted(down_right, -1)
    near = own[:, cols + HD :]
    near = jnp.concatenate([near] + [shifted(near, turn, "yl") for turn in (1, 2, 3)], axis=0)
    far = partner(near, "c")
    queries = gathered(own[:, : cols + HD], "z").reshape(-1, cols + HD)

    packed = local(attend, shape((queries.shape[0], cols + HD)), queries, near, far)
    packed = exchange(packed.reshape(n_z, rows, cols + HD), "z")

    partial = local(project, shape((n_x, 2 * tok, width)), packed, out_weight)
    parts = exchange(partial, "x")
    gated = jnp.sum(parts.astype(F32), axis=0) * gate
    first = where[0] == 0
    ours = jnp.where(first, gated[:tok], gated[tok:]) + residual.astype(F32)
    message = jnp.concatenate(
        [jnp.where(first, ours, gated[:tok]), jnp.where(first, gated[tok:], ours)], axis=0
    ).astype(BF16)
    middle, near = local(
        normalize,
        (shape((tok, width), F32), shape((2 * tok, width + LANES))),
        where,
        gated,
        partner(message, "yh"),
        residual,
        shift,
        factor,
        own,
        smem=(0,),
    )
    far = partner(near, "c")

    buffer_rows = n_plane * 4 * SLOTS
    sent = local(dispatch, shape((buffer_rows, width)), where, near, far, smem=(0,))
    arrived = exchange(sent.reshape(n_plane, -1, width), PLANE).reshape(buffer_rows, width)
    ups, downs = (up, up_left, up_right, up_far), (down, down_left, down_right, down_far)
    output = local(
        run_expert,
        shape((buffer_rows, width)),
        arrived,
        *ups,
        *downs,
        elsewhere=range(1, 1 + 2 * n_x),
        scratch_shapes=[
            pltpu.VMEM((n_x, *up.shape), BF16),
            pltpu.VMEM((n_x, *down.shape), BF16),
            pltpu.SemaphoreType.DMA((2, n_x)),
        ],
    )
    returned = exchange(output.reshape(n_plane, -1, width), PLANE).reshape(buffer_rows, width)

    kept, given = local(
        mix,
        (shape((2 * tok, width), F32), shape((2 * tok, width))),
        where,
        near,
        far,
        returned,
        smem=(0,),
    )
    both = kept + partner(given, "c").astype(F32)
    low, high = both[:tok], both[tok:]
    given = jnp.where(first, high, low).astype(BF16)
    mixture = jnp.where(first, low, high) + partner(given, "yh").astype(F32)
    return (middle + expert_gate * mixture).astype(BF16)


def solution(mesh):
    split = Mesh(mesh.devices.reshape(2, 4, 4, 8, 2), AXES)
    everywhere = P(AXES, None)
    placed = (
        everywhere,
        everywhere,
        everywhere,
        everywhere,
        P(HEAD, None),
        P(),
        P(),
        P(),
        P(),
        P(BLK, None, HEAD),
        P(BLK, HEAD, None),
        everywhere,
        everywhere,
    )
    return jax.shard_map(layer, mesh=split, in_specs=placed, out_specs=everywhere, check_vma=False)
```

```python
import math

import jax
import jax.numpy as jnp
from jax import lax
from jax.experimental import pallas as pl
from jax.experimental.pallas import tpu as pltpu
from jax.sharding import Mesh
from jax.sharding import PartitionSpec as P

HD = 64
TOPK = 2
SLOTS = 2
LANES = 128
AXES = ("yh", "x", "yl", "z", "c")
HEAD = ("yh", "x")
BLK = ("yl", "z", "c")
PLANE = ("yl", "z")
BF16 = jnp.bfloat16
F32 = jnp.float32
RATE = math.log2(math.e) / math.sqrt(HD)


def exchange(array, axis):
    return lax.all_to_all(array, axis, 0, 0, tiled=True)


def gathered(array, axis):
    copies = jnp.broadcast_to(array[None], (lax.axis_size(axis), *array.shape))
    return exchange(copies, axis)


def partner(array, axis):
    return lax.ppermute(array, axis, [(0, 1), (1, 0)])


def shifted(array, by, axis="x"):
    n = lax.axis_size(axis)
    return lax.ppermute(array, axis, [(i, (i + by) % n) for i in range(n)])


def iota(shape, dim):
    return lax.broadcasted_iota(jnp.int32, shape, dim)


def dot(a, b, dims=((1,), (0,))):
    return lax.dot_general(a, b, (dims, ((), ())), preferred_element_type=F32)


def pieces(values):
    out = []
    for _ in range(3):
        piece = values.astype(BF16).astype(F32)
        out.append(piece)
        values = values - piece
    return out


def local(body, outs, *args, smem=(), elsewhere=(), **kw):
    specs, placed = [], []
    for i, arg in enumerate(args):
        if i in smem:
            specs.append(pl.BlockSpec(memory_space=pltpu.SMEM))
        elif i in elsewhere:
            specs.append(pl.BlockSpec(memory_space=pl.ANY))
        else:
            specs.append(pl.BlockSpec(memory_space=pltpu.VMEM))
            arg = pltpu.with_memory_space_constraint(arg, pltpu.VMEM)
        placed.append(arg)
    return pl.pallas_call(
        body,
        out_shape=jax.tree.map(lambda o: pltpu.VMEM(o.shape, o.dtype), outs),
        in_specs=specs,
        out_specs=jax.tree.map(lambda _: pl.BlockSpec(memory_space=pltpu.VMEM), outs),
        **kw,
    )(*placed)


def shape(dims, kind=BF16):
    return jax.ShapeDtypeStruct(dims, kind)


def prepare(q_ref, k_ref, v_ref, route_ref, weight_ref, out_ref):
    groups, tok, _ = out_ref.shape
    cols = q_ref.shape[1] // groups
    weight = weight_ref[...]
    lines = [route_ref[k : k + 1, :].astype(F32) for k in range(TOPK)]
    for piece in pieces(weight):
        lines += [piece[k : k + 1, :] for k in range(TOPK)]
    row = iota((16, tok), 0)
    table = jnp.zeros((16, tok), F32)
    for i, line in enumerate(lines):
        table = jnp.where(row == i, line, table)
    pick = (iota((16, HD), 0) == iota((16, HD), 1)).astype(BF16)
    header = dot(table.astype(BF16), pick, ((0,), (0,))).astype(BF16)
    for g in range(groups):
        span = slice(g * cols, (g + 1) * cols)
        out_ref[g] = jnp.concatenate(
            [q_ref[:, span], header, k_ref[:, span], v_ref[:, span]], axis=1
        )


def attend(own_ref, other_ref, keys_ref, own_out_ref, other_out_ref):
    wide = own_ref.shape[1]
    cols, rows = wide - HD, 256
    half = keys_ref.shape[0] // 2
    near_k, far_k = keys_ref[:half, :cols], keys_ref[half:, :cols]
    near_v, far_v = keys_ref[:half, LANES:], keys_ref[half:, LANES:]
    q_head = iota((rows, cols), 1) // HD
    o_head = iota((rows, wide), 1) // HD - 1
    lane = iota((rows, LANES), 1)
    blocks = [(other_ref, other_out_ref), (own_ref, own_out_ref)]
    blocks = [(*refs, at) for refs in blocks for at in range(0, own_ref.shape[0], rows)]
    for q_ref, out_ref, start in blocks:
        q = q_ref[start : start + rows, :cols]
        out = jnp.zeros((rows, wide), F32)
        stats = jnp.zeros((rows, LANES), F32)
        for j in range(cols // HD):
            q_j = jnp.where(q_head == j, q, jnp.zeros_like(q))
            near = dot(q_j, near_k, ((1,), (1,)))
            far = dot(q_j, far_k, ((1,), (1,)))
            peak = jnp.maximum(
                jnp.max(near, axis=1, keepdims=True), jnp.max(far, axis=1, keepdims=True)
            )
            near = jnp.exp2((near - peak) * RATE)
            far = jnp.exp2((far - peak) * RATE)
            total = jnp.sum(near, axis=1, keepdims=True) + jnp.sum(far, axis=1, keepdims=True)
            accum = dot(near.astype(BF16), near_v) + dot(far.astype(BF16), far_v)
            out = jnp.where(o_head == j, accum * (1.0 / total), out)
            for i, piece in enumerate(pieces(peak) + pieces(total)):
                stats = jnp.where(lane == 6 * j + i, piece, stats)
        stats = jnp.where(lane < HD, stats, out[:, :LANES])
        out_ref[start : start + rows, :LANES] = stats.astype(BF16)
        out_ref[start : start + rows, LANES:] = out[:, LANES:].astype(BF16)


def project(*refs):
    *part_refs, weight_ref, out_ref = refs
    n_x, pair_rows, _ = out_ref.shape
    tok = pair_rows // 2
    rows, wide = n_x * pair_rows, part_refs[0].shape[1]
    parts = jnp.concatenate([ref[...] for ref in part_refs], axis=0)
    count = parts.shape[0] // rows
    stats = parts[:, :LANES]
    parts = parts.reshape(count, rows, wide)
    src = iota((LANES, wide), 0)
    head = jnp.maximum(iota((LANES, wide), 1) // HD - 1, 0)
    at = src - 6 * head
    peak = dot(stats, ((at >= 0) & (at < 3)).astype(BF16)).reshape(count, rows, wide)
    total = dot(stats, ((at >= 3) & (at < 6)).astype(BF16)).reshape(count, rows, wide)
    top = jnp.max(peak, axis=0)
    share = total * jnp.exp2((peak - top[None]) * RATE)
    numer = jnp.sum(share * parts.astype(F32), axis=0)
    attended = (numer / jnp.sum(share, axis=0))[:, HD:].astype(BF16)
    projected = dot(attended, weight_ref[...]).astype(BF16)
    for side in range(2):
        for x in range(n_x):
            start = (side * n_x + x) * tok
            out_ref[x, side * tok : (side + 1) * tok, :] = projected[start : start + tok]


def normalize(
    where_ref, sum_ref, got_ref, residual_ref, shift_ref, factor_ref, middle_ref, out_ref
):
    tok = residual_ref.shape[0]
    own = where_ref[0]
    residual = residual_ref[...].astype(F32)
    for side in range(2):
        span = slice(side * tok, (side + 1) * tok)
        added = jnp.where(own == side, residual, 0.0)
        middle = sum_ref[span, :] + got_ref[span, :].astype(F32) + added

        @pl.when(own == side)
        def _():
            middle_ref[...] = middle

        average = jnp.mean(middle, axis=1, keepdims=True)
        centered = middle - average
        variance = jnp.mean(centered * centered, axis=1, keepdims=True)
        scaled = centered * lax.rsqrt(variance + 1e-06) * factor_ref[...]
        out_ref[span, :] = (scaled + shift_ref[...]).astype(BF16)


def pair_headers(where_ref, own_ref, out_ref):
    tok = out_ref.shape[0] // 2
    n_x = own_ref.shape[0] // (2 * tok)
    for side in range(2):
        start = pl.multiple_of((side * n_x + where_ref[1]) * tok, tok)
        out_ref[side * tok : (side + 1) * tok, :] = own_ref[pl.ds(start, tok), LANES : 2 * LANES]


def places(near_ref, far_ref, c, across):
    pair = near_ref.shape[0]
    tok = pair // 2
    count = 2 * pair
    headers = jnp.concatenate([near_ref[...], far_ref[...]], axis=0)
    take = (iota((8, LANES), 1) == iota((8, LANES), 0) + HD).astype(BF16)
    lines = dot(take, headers, ((1,), (1,)))
    headers = headers.astype(F32)
    lane = iota((count, LANES), 1)

    def column(i):
        return jnp.sum(jnp.where(lane == HD + i, headers, 0.0), axis=1, keepdims=True)

    line = [lines[k : k + 1, :] for k in range(TOPK)]
    col = [column(k) for k in range(TOPK)]
    named, others, axis = (line, col, 0) if across else (col, line, 1)
    this, other = iota((count, count), 1 - axis), iota((count, count), axis)
    before = (other < this) & (this // tok == other // tok)
    group = iota((1, count), 1) // tok if across else iota((count, 1), 0) // tok
    out = []
    for k in range(TOPK):
        same = sum((other_k == named[k]).astype(F32) for other_k in others)
        slot = jnp.sum(jnp.where(before, same, 0.0), axis=axis, keepdims=True).astype(jnp.int32)
        expert = named[k].astype(jnp.int32)
        place = (expert // 2) * (4 * SLOTS) + group * SLOTS + slot
        out.append(jnp.where(expert % 2 == c, place, -1))
    return out, column


def plan(where_ref, near_ref, far_ref, send_ref, pick_ref):
    rows, count = send_ref.shape
    chosen, _ = places(near_ref, far_ref, where_ref[2], True)
    target = iota((rows, count), 0)
    send_ref[...] = sum((target == place).astype(F32) for place in chosen).astype(BF16)
    chosen, column = places(near_ref, far_ref, where_ref[2], False)
    source = iota((count, rows), 1)
    pick = jnp.zeros((count, rows), F32)
    for k, place in enumerate(chosen):
        weight = sum(column(TOPK * (1 + i) + k) for i in range(3))
        pick = pick + jnp.where(source == place, weight, 0.0)
    high, low, _ = pieces(pick)
    pick_ref[:count] = high.astype(BF16)
    pick_ref[count:] = low.astype(BF16)


def dispatch(send_ref, near_ref, far_ref, out_ref):
    pair = near_ref.shape[0]
    out_ref[...] = (
        dot(send_ref[:, :pair], near_ref[...]) + dot(send_ref[:, pair:], far_ref[...])
    ).astype(BF16)


def run_expert(rows_ref, *refs):
    *weights, out_ref, up_buf, down_buf, sem = refs
    count = len(weights) // 2
    ups, downs = weights[:count], weights[count:]
    copies = []
    for i in range(count):
        copies.append(
            (
                pltpu.make_async_copy(ups[i], up_buf.at[i], sem.at[0, i]),
                pltpu.make_async_copy(downs[i], down_buf.at[i], sem.at[1, i]),
            )
        )
        for copy in copies[-1]:
            copy.start()
    rows = rows_ref[...]
    total = jnp.zeros(out_ref.shape, F32)
    for i in range(count):
        copies[i][0].wait()
        hidden = jax.nn.gelu(dot(rows, up_buf[i]), approximate=True).astype(BF16)
        copies[i][1].wait()
        total = total + dot(hidden, down_buf[i])
    out_ref[...] = total.astype(BF16)


def mix(pick_ref, rows_ref, kept_ref, given_ref):
    pair = kept_ref.shape[0]
    mixed = dot(pick_ref[...], rows_ref[...])
    mixed = mixed[: 2 * pair] + mixed[2 * pair :]
    kept_ref[...] = mixed[:pair]
    given_ref[...] = mixed[pair:].astype(BF16)


def layer(
    query_rows,
    key_rows,
    value_rows,
    residual,
    out_weight,
    attention_gate,
    norm_shift,
    norm_scale,
    expert_gate,
    expert_up,
    expert_down,
    routing,
    combine_weight,
):
    tok, width = query_rows.shape
    n_head = lax.axis_size(HEAD)
    n_x = lax.axis_size("x")
    n_plane = lax.axis_size(PLANE)
    cols = width // n_head
    rows = n_head * tok
    where = jnp.stack([lax.axis_index(a) for a in ("yh", "x", "c")]).astype(jnp.int32)
    factor = (1.0 + norm_scale).reshape(1, width)
    gate = attention_gate.reshape(1, width)
    shift = norm_shift.reshape(1, width)

    own = pl.pallas_call(
        prepare, out_shape=pltpu.VMEM((n_head, tok, 3 * cols + HD), BF16), name="prepare"
    )(query_rows, key_rows, value_rows, routing.T, combine_weight.T)
    own = exchange(own, HEAD).reshape(rows, 3 * cols + HD)

    up, down = expert_up[0], expert_down[0]
    up_left, down_left = shifted(up, 1), shifted(down, 1)
    up_right, down_right = shifted(up, -1), shifted(down, -1)
    up_far = shifted(up_left, 1)
    down_far = shifted(down_right, -1)
    keys = gathered(own[:, cols + HD :], "z").reshape(-1, 2 * cols)
    queries = own[:, : cols + HD]
    turns = range(1, lax.axis_size("yl"))
    queries = jnp.concatenate([queries] + [shifted(queries, t, "yl") for t in turns], axis=0)
    near, far = local(
        attend, (shape(queries.shape), shape(queries.shape)), queries, partner(queries, "c"), keys
    )
    far = partner(far, "c")
    parts = [
        jnp.concatenate([a[t * rows : (t + 1) * rows] for a in (near, far)], axis=0)
        for t in range(1 + len(turns))
    ]
    parts = parts[:1] + [shifted(parts[t], -t, "yl") for t in turns]

    buffer_rows = n_plane * 4 * SLOTS
    near = local(pair_headers, shape((2 * tok, LANES)), where, own, smem=(0,))
    far = partner(near, "c")
    send, pick = local(
        plan,
        (shape((buffer_rows, 4 * tok)), shape((8 * tok, buffer_rows))),
        where,
        near,
        far,
        smem=(0,),
    )

    partial = local(project, shape((n_x, 2 * tok, width)), *parts, out_weight)
    parts = exchange(partial, "x")
    gated = jnp.sum(parts.astype(F32), axis=0) * gate
    first = where[0] == 0
    ours = jnp.where(first, gated[:tok], gated[tok:]) + residual.astype(F32)
    message = jnp.concatenate(
        [jnp.where(first, ours, gated[:tok]), jnp.where(first, gated[tok:], ours)], axis=0
    ).astype(BF16)
    got = partner(message, "yh")
    middle, near = local(
        normalize,
        (shape((tok, width), F32), shape((2 * tok, width))),
        where,
        gated,
        got,
        residual,
        shift,
        factor,
        smem=(0,),
    )
    far = partner(near, "c")

    sent = local(dispatch, shape((buffer_rows, width)), send, near, far)
    arrived = exchange(sent.reshape(n_plane, -1, width), PLANE).reshape(buffer_rows, width)
    ups, downs = (up, up_left, up_right, up_far), (down, down_left, down_right, down_far)
    output = local(
        run_expert,
        shape((buffer_rows, width)),
        arrived,
        *ups,
        *downs,
        elsewhere=range(1, 1 + 2 * n_x),
        scratch_shapes=[
            pltpu.VMEM((n_x, *up.shape), BF16),
            pltpu.VMEM((n_x, *down.shape), BF16),
            pltpu.SemaphoreType.DMA((2, n_x)),
        ],
    )
    returned = exchange(output.reshape(n_plane, -1, width), PLANE).reshape(buffer_rows, width)

    kept, given = local(
        mix, (shape((2 * tok, width), F32), shape((2 * tok, width))), pick, returned
    )
    both = kept + partner(given, "c").astype(F32)
    low, high = both[:tok], both[tok:]
    given = jnp.where(first, high, low).astype(BF16)
    mixture = jnp.where(first, low, high) + partner(given, "yh").astype(F32)
    return (middle + expert_gate * mixture).astype(BF16)


def solution(mesh):
    split = Mesh(mesh.devices.reshape(2, 4, 4, 8, 2), AXES)
    everywhere = P(AXES, None)
    placed = (
        everywhere,
        everywhere,
        everywhere,
        everywhere,
        P(HEAD, None),
        P(),
        P(),
        P(),
        P(),
        P(BLK, None, HEAD),
        P(BLK, HEAD, None),
        everywhere,
        everywhere,
    )
    return jax.shard_map(layer, mesh=split, in_specs=placed, out_specs=everywhere, check_vma=False)
```
